128 devices in a mesh: req: 32 (over y, x, core), mlp: 4 (over z).
Axes of the slice: x: 4, y: 4, z: 4, core: 2. Of those that a mesh axis runs over, the one named last changes fastest.
Arguments:
- states: bfloat16 [8192, 2560], P('req')
- attn_gain: float32 [2560], replicated, may hold values from 0.1 to 1.9
- query_matrix: bfloat16 [2560, 2048], P(None, 'mlp')
- key_matrix: bfloat16 [2560, 1024], P(None, 'mlp')
- value_matrix: bfloat16 [2560, 1024], P(None, 'mlp'), may hold values from -0.125 to 0.125
- query_gain: float32 [256], replicated
- key_gain: float32 [256], replicated
- out_weight: bfloat16 [2048, 2560], P('mlp'), may hold values from -0.125 to 0.125
- post_gain: float32 [2560], replicated, may hold values from 0.1 to 1.9
- ffw_gain: float32 [2560], replicated, may hold values from 0.1 to 1.9
- gate_weight: bfloat16 [2560, 10240], P(None, 'req'), may hold values from -0.125 to 0.125
- up_weight: bfloat16 [2560, 10240], P(None, 'req'), may hold values from -0.125 to 0.125
- down_weight: bfloat16 [10240, 2560], P('req'), may hold values from -0.0625 to 0.0625
- post_ffw_gain: float32 [2560], replicated, may hold values from 0.1 to 1.9
- prefix_key_cache: bfloat16 [32, 512, 1024], P('req', None, 'mlp')
- prefix_value_cache: bfloat16 [32, 512, 1024], P('req', None, 'mlp'), may hold values from -6 to 6
- segment: int32 [8192], P('req'), may hold values from 0 to 15, as said below
- prefix_id: int32 [8192], P('req'), may hold values from 0 to 31, as said below
- owner_map: int32 [32], replicated, may hold values from 0 to 31, each once
Outputs:
- layer_out: bfloat16 [8192, 2560], P(('req', 'mlp'))
The draws below stay inside these ranges and needn't reach their ends.
Inputs may be any that keep to these rules, and one draw needn't show every extreme that they name: Within each block of 256 rows, equal segment values mark one request and occupy contiguous rows; requests hold 16 or 32 tokens. `prefix_id`: all tokens of one request name the same prefix group. In each block of 256 rows at most 32 rows name prefix groups of the same owner, and one prefix group is named by exactly 32 rows of every block.
All inputs are finite; a program needn't handle non-finite values.
Results may differ from the reference program's by a relative error of at most 0.017.
The reference program's roundings to bfloat16 on the way count: a program that leaves them out, or rounds other values in their place, can miss the bound.
Values may be sent and summed in bfloat16 or wider, within the bound.
A program may use at most 128 MiB of HBM per device.

```python
import math
import jax
import jax.numpy as jnp
from jax import lax

MODEL_WIDTH = 2560
FF = 10240
QUERY_HEADS = 8
KEY_VALUE_HEADS = 4
HEAD_SIZE = 256
TOKENS_PER_REQ = 256
PREFIX_LENGTH = 512
CAP = 32
SUFFIX_TOKENS = 8192
PREFIX_NUMBER = 32


def draw_states(key, part):
    sampled_items = jnp.clip(jax.random.normal(jax.random.fold_in(key, 101), (SUFFIX_TOKENS, MODEL_WIDTH), jnp.float32), -6.0, 6.0)
    return sampled_items.astype(jnp.bfloat16)


def draw_query_matrix(key, part):
    sampled_items = jax.random.normal(jax.random.fold_in(key, 201), (MODEL_WIDTH, QUERY_HEADS * HEAD_SIZE), jnp.float32)
    return (sampled_items / math.sqrt(MODEL_WIDTH)).astype(jnp.bfloat16)


def draw_key_matrix(key, part):
    sampled_items = jax.random.normal(jax.random.fold_in(key, 301), (MODEL_WIDTH, KEY_VALUE_HEADS * HEAD_SIZE), jnp.float32)
    return (sampled_items / math.sqrt(MODEL_WIDTH)).astype(jnp.bfloat16)


def draw_query_gain(key, part):
    return jax.random.uniform(jax.random.fold_in(key, 401), (HEAD_SIZE,), jnp.float32, 0.6, 1.6)


def draw_key_gain(key, part):
    return jax.random.uniform(jax.random.fold_in(key, 501), (HEAD_SIZE,), jnp.float32, 0.6, 1.6)


def draw_prefix_key_cache(key, part):
    sampled_items = jnp.clip(jax.random.normal(jax.random.fold_in(key, 601), (PREFIX_NUMBER, PREFIX_LENGTH, KEY_VALUE_HEADS * HEAD_SIZE), jnp.float32), -6.0, 6.0)
    return sampled_items.astype(jnp.bfloat16)


def request_layout(key):
    base = jax.random.fold_in(key, 777)
    device_count = SUFFIX_TOKENS // TOKENS_PER_REQ
    block_count = TOKENS_PER_REQ // CAP
    hot_group = jax.random.randint(jax.random.fold_in(base, 1), (), 0, PREFIX_NUMBER)
    device_keys = jax.random.split(jax.random.fold_in(base, 2), device_count)
    others = jax.vmap(lambda one_key: jax.random.permutation(one_key, PREFIX_NUMBER - 1))(device_keys)[:, :block_count - 1]
    others = others + (others >= hot_group).astype(others.dtype)
    hot_at = jax.random.randint(jax.random.fold_in(base, 3), (device_count,), 0, block_count)
    block_index = jnp.arange(block_count, dtype=jnp.int32)
    pick = jnp.clip(block_index[None, :] - (block_index[None, :] > hot_at[:, None]).astype(jnp.int32), 0, block_count - 2)
    chosen = jnp.take_along_axis(others, pick, axis=1)
    block_group = jnp.where(block_index[None, :] == hot_at[:, None], hot_group, chosen)
    split_flag = jax.random.randint(jax.random.fold_in(base, 4), (device_count, block_count), 0, 2)
    offset = jnp.arange(CAP, dtype=jnp.int32)
    seg_ids = 2 * block_index[None, :, None] + split_flag[:, :, None] * (offset[None, None, :] >= CAP // 2).astype(jnp.int32)
    group_ids = jnp.broadcast_to(block_group[:, :, None], (device_count, block_count, CAP))
    return (seg_ids.reshape(SUFFIX_TOKENS).astype(jnp.int32), group_ids.reshape(SUFFIX_TOKENS).astype(jnp.int32))


def draw_segment(key, part):
    return request_layout(key)[0]


def draw_prefix_id(key, part):
    return request_layout(key)[1]


def levels(rng, shape, cuts, smallest, high):
    gain, own = 1.0, jax.random.fold_in(rng, 6)
    for axis_at, blocks in cuts:
        draws = jnp.exp(jax.random.uniform(jax.random.fold_in(own, axis_at), (blocks,), jnp.float32, smallest / len(cuts), high / len(cuts)))
        gain = gain * jnp.repeat(draws, shape[axis_at] // blocks).reshape([-1 if axis == axis_at else 1 for axis in range(len(shape))])
    return gain


def normal_values(key, extent, deviation, reach, shards=(), held_as=jnp.bfloat16):
    factor_of = levels(key, extent, shards, -0.22, 0.18) if shards else 1.0
    drawn = jax.random.normal(key, extent, jnp.float32) * deviation * factor_of
    return jnp.minimum(jnp.maximum(drawn, -reach), reach).astype(held_as)


def setup_inputs(seed: int = 0) -> dict:
    keys = jax.random.split(jax.random.key(seed), 20)
    return {
        "states": draw_states(jax.random.fold_in(keys[19], 71), 0),
        "attn_gain": jnp.clip(1.0 + 0.18 * jax.random.normal(keys[1], (MODEL_WIDTH,), jnp.float32), 0.1, 1.9),
        "query_matrix": draw_query_matrix(jax.random.fold_in(keys[19], 71), 0),
        "key_matrix": draw_key_matrix(jax.random.fold_in(keys[19], 71), 0),
        "value_matrix": normal_values(keys[4], (MODEL_WIDTH, KEY_VALUE_HEADS * HEAD_SIZE), MODEL_WIDTH ** -0.5, 0.125, ((1, 4),)),
        "query_gain": draw_query_gain(jax.random.fold_in(keys[19], 71), 0),
        "key_gain": draw_key_gain(jax.random.fold_in(keys[19], 71), 0),
        "out_weight": normal_values(keys[7], (QUERY_HEADS * HEAD_SIZE, MODEL_WIDTH), (QUERY_HEADS * HEAD_SIZE) ** -0.5, 0.125, ((0, 4),)),
        "post_gain": jnp.clip(1.0 + 0.18 * jax.random.normal(keys[8], (MODEL_WIDTH,), jnp.float32), 0.1, 1.9),
        "ffw_gain": jnp.clip(1.0 + 0.18 * jax.random.normal(keys[9], (MODEL_WIDTH,), jnp.float32), 0.1, 1.9),
        "gate_weight": normal_values(keys[10], (MODEL_WIDTH, FF), MODEL_WIDTH ** -0.5, 0.125, ((1, 32),)),
        "up_weight": normal_values(keys[11], (MODEL_WIDTH, FF), MODEL_WIDTH ** -0.5, 0.125, ((1, 32),)),
        "down_weight": normal_values(keys[12], (FF, MODEL_WIDTH), FF ** -0.5, 0.0625, ((0, 32),)),
        "post_ffw_gain": jnp.clip(1.0 + 0.18 * jax.random.normal(keys[13], (MODEL_WIDTH,), jnp.float32), 0.1, 1.9),
        "prefix_key_cache": draw_prefix_key_cache(jax.random.fold_in(keys[19], 71), 0),
        "prefix_value_cache": normal_values(keys[15], (PREFIX_NUMBER, PREFIX_LENGTH, KEY_VALUE_HEADS * HEAD_SIZE), 1.0, 6.0, ((0, 32), (2, 4))),
        "segment": draw_segment(jax.random.fold_in(keys[19], 71), 0),
        "prefix_id": draw_prefix_id(jax.random.fold_in(keys[19], 71), 0),
        "owner_map": jax.random.permutation(keys[18], PREFIX_NUMBER).astype(jnp.int32),
    }


EPS = 1e-06

def normed(values_in, gain_vec):
    return values_in * lax.rsqrt(lax.optimization_barrier(jnp.mean(values_in * values_in, axis=-1, keepdims=True)) + EPS) * gain_vec

def widened(array_in):
    return lax.optimization_barrier(array_in.astype(jnp.bfloat16)).astype(jnp.float32)

def local_attention(query_rows, key_rows, value_rows, segment_rows, score_scale):
    scores = jnp.einsum('tgqd,sgd->gqts', query_rows.astype(jnp.float32), key_rows.astype(jnp.float32)) * score_scale
    row_count = segment_rows.shape[0]
    token_position = jnp.arange(row_count, dtype=jnp.int32)
    allowed = (segment_rows[:, None] == segment_rows[None, :]) & (token_position[:, None] >= token_position[None, :])
    scores = jnp.where(allowed, scores, -jnp.inf)
    row_max = lax.optimization_barrier(jnp.max(scores, axis=-1, keepdims=True))
    powers = jnp.exp(scores - row_max)
    row_sum = lax.optimization_barrier(jnp.sum(powers, axis=-1, keepdims=True))
    weights = widened(powers / row_sum)
    mixed = jnp.einsum('gqts,sgd->tgqd', weights, value_rows.astype(jnp.float32))
    log_total = jnp.transpose((row_max + jnp.log(row_sum))[..., 0], (2, 0, 1))
    return (mixed, log_total)

def reference(states, attn_gain, query_matrix, key_matrix, value_matrix, query_gain, key_gain, out_weight, post_gain, ffw_gain, gate_weight, up_weight, down_weight, post_ffw_gain, prefix_key_cache, prefix_value_cache, segment, prefix_id, owner_map):
    query_group_width = QUERY_HEADS // KEY_VALUE_HEADS
    score_scale = 1.0 / math.sqrt(HEAD_SIZE)
    block_list = SUFFIX_TOKENS // TOKENS_PER_REQ
    states_f = states.astype(jnp.float32)
    normalized_input = normed(states_f, attn_gain).astype(jnp.bfloat16)
    unnormed_queries = jnp.dot(normalized_input, query_matrix, preferred_element_type=jnp.float32).reshape(SUFFIX_TOKENS, KEY_VALUE_HEADS, query_group_width, HEAD_SIZE)
    query_vectors = normed(unnormed_queries, query_gain).astype(jnp.bfloat16)
    unnormed_keys = jnp.dot(normalized_input, key_matrix, preferred_element_type=jnp.float32).reshape(SUFFIX_TOKENS, KEY_VALUE_HEADS, HEAD_SIZE)
    key_vectors = normed(unnormed_keys, key_gain).astype(jnp.bfloat16)
    value_vectors = jnp.dot(normalized_input, value_matrix, preferred_element_type=jnp.float32).astype(jnp.bfloat16).reshape(SUFFIX_TOKENS, KEY_VALUE_HEADS, HEAD_SIZE)

    def single_block(pieces):
        return local_attention(pieces[0], pieces[1], pieces[2], pieces[3], score_scale)
    suffix_output, suffix_log_sum = lax.map(single_block, (query_vectors.reshape(block_list, TOKENS_PER_REQ, KEY_VALUE_HEADS, query_group_width, HEAD_SIZE), key_vectors.reshape(block_list, TOKENS_PER_REQ, KEY_VALUE_HEADS, HEAD_SIZE), value_vectors.reshape(block_list, TOKENS_PER_REQ, KEY_VALUE_HEADS, HEAD_SIZE), segment.reshape(block_list, TOKENS_PER_REQ)))
    suffix_output = suffix_output.reshape(SUFFIX_TOKENS, KEY_VALUE_HEADS, query_group_width, HEAD_SIZE)
    suffix_log_sum = suffix_log_sum.reshape(SUFFIX_TOKENS, KEY_VALUE_HEADS, query_group_width)
    cache_row = owner_map[prefix_id].astype(jnp.int32)
    query_f = query_vectors.astype(jnp.float32)

    def visit(carry, selected_index):
        stored_keys = prefix_key_cache[selected_index].astype(jnp.float32).reshape(PREFIX_LENGTH, KEY_VALUE_HEADS, HEAD_SIZE)
        stored_values = prefix_value_cache[selected_index].astype(jnp.float32).reshape(PREFIX_LENGTH, KEY_VALUE_HEADS, HEAD_SIZE)
        scores = jnp.einsum('tgqd,kgd->tgqk', query_f, stored_keys) * score_scale
        row_max = lax.optimization_barrier(jnp.max(scores, axis=-1, keepdims=True))
        powers = jnp.exp(scores - row_max)
        row_sum = lax.optimization_barrier(jnp.sum(powers, axis=-1, keepdims=True))
        weights = widened(powers / row_sum)
        mixed = widened(jnp.einsum('tgqk,kgd->tgqd', weights, stored_values))
        log_total = row_max[..., 0] + jnp.log(row_sum[..., 0])
        chosen = cache_row == selected_index
        new_out = jnp.where(chosen[:, None, None, None], mixed, carry[0])
        new_lse = jnp.where(chosen[:, None, None], log_total, carry[1])
        return ((new_out, new_lse), None)
    initial_state = (jnp.zeros((SUFFIX_TOKENS, KEY_VALUE_HEADS, query_group_width, HEAD_SIZE), jnp.float32), jnp.zeros((SUFFIX_TOKENS, KEY_VALUE_HEADS, query_group_width), jnp.float32))
    (prefix_out, prefix_lse), _ = lax.scan(visit, initial_state, jnp.arange(PREFIX_NUMBER, dtype=jnp.int32))
    blend = jax.nn.sigmoid(prefix_lse - suffix_log_sum)[..., None]
    attended = (blend * prefix_out + (1.0 - blend) * suffix_output).astype(jnp.bfloat16).reshape(SUFFIX_TOKENS, QUERY_HEADS * HEAD_SIZE)
    attn_sum = jnp.dot(attended, out_weight, preferred_element_type=jnp.float32)
    residual = states_f + normed(attn_sum, post_gain)
    ffw_in = normed(residual, ffw_gain).astype(jnp.bfloat16)
    gate_proj = jnp.dot(ffw_in, gate_weight, preferred_element_type=jnp.float32)
    up_proj = jnp.dot(ffw_in, up_weight, preferred_element_type=jnp.float32)
    hidden = (jax.nn.gelu(gate_proj, approximate=True) * up_proj).astype(jnp.bfloat16)
    down_sum = jnp.dot(hidden, down_weight, preferred_element_type=jnp.float32)
    return (residual + normed(down_sum, post_ffw_gain)).astype(jnp.bfloat16)
```

```python
import jax
import jax.numpy as jnp
from jax import lax
from jax.experimental import pallas as pl
from jax.experimental.pallas import tpu as pltpu
from jax.sharding import PartitionSpec as P

CAP = 32


EPS = 1e-06


def normed(values_in, gain_vec):
    return (
        values_in
        * lax.rsqrt(jnp.mean(values_in * values_in, axis=-1, keepdims=True) + EPS)
        * gain_vec
    )


def local_attention(query_rows, key_rows, value_rows, segment_rows, score_scale):
    scores = (
        jnp.einsum("tgqd,sgd->gqts", query_rows, key_rows, preferred_element_type=jnp.float32)
        * score_scale
    )
    row_count = segment_rows.shape[0]
    token_position = jnp.arange(row_count, dtype=jnp.int32)
    allowed = (segment_rows[:, None] == segment_rows[None, :]) & (
        token_position[:, None] >= token_position[None, :]
    )
    scores = jnp.where(allowed, scores, -jnp.inf)
    row_max = jnp.max(scores, axis=-1, keepdims=True)
    powers = jnp.exp(scores - row_max)
    row_sum = jnp.sum(powers, axis=-1, keepdims=True)
    weights = (powers / row_sum).astype(jnp.bfloat16)
    mixed = jnp.einsum("gqts,sgd->tgqd", weights, value_rows, preferred_element_type=jnp.float32)
    log_total = jnp.transpose((row_max + jnp.log(row_sum))[..., 0], (2, 0, 1))
    return (mixed, log_total)


def prefix_partials(incoming, stored_keys, stored_values, score_scale):
    sources, slot_count, head_cols = incoming.shape
    kv_heads = stored_keys.shape[1]
    head_dim = stored_keys.shape[2]
    query_group_width = head_cols // (kv_heads * head_dim)
    query_rows = incoming.reshape(sources * slot_count, kv_heads, query_group_width, head_dim)
    scores = (
        jnp.einsum("rgqd,kgd->rgqk", query_rows, stored_keys, preferred_element_type=jnp.float32)
        * score_scale
    )
    row_max = jnp.max(scores, axis=-1, keepdims=True)
    powers = jnp.exp(scores - row_max)
    row_sum = jnp.sum(powers, axis=-1, keepdims=True)
    weights = (powers / row_sum).astype(jnp.bfloat16)
    mixed = jnp.einsum("rgqk,kgd->rgqd", weights, stored_values, preferred_element_type=jnp.float32)
    mixed = lax.optimization_barrier(mixed.astype(jnp.bfloat16)).astype(jnp.float32)
    log_total = row_max[..., 0] + jnp.log(row_sum[..., 0])
    return (
        mixed.reshape(sources, slot_count, head_cols),
        log_total.reshape(sources, slot_count, kv_heads * query_group_width),
    )


MESH_ID = pl.DeviceIdType.MESH
RING = 4
SUB = 32
HALF = 16


def torus_place():
    me = lax.axis_index("req")
    layer = lax.axis_index("mlp")
    core = lax.rem(me, 2)
    chip = me // 2
    col = lax.rem(chip, RING)
    row = chip // RING

    def at(row_at, col_at, core_at):
        return ((row_at * RING + col_at) * 2 + core_at, layer)

    up = at(lax.rem(row + 1, RING), col, core)
    down = at(lax.rem(row + RING - 1, RING), col, core)
    right = at(row, lax.rem(col + 1, RING), core)
    left = at(row, lax.rem(col + RING - 1, RING), core)
    sibling = at(row, col, 1 - core)
    return right, left, up, down, sibling


def ffn_kernel(
    ffw_in_ref,
    residual_ref,
    gain_ref,
    gate_ref,
    up_ref,
    down_ref,
    out_ref,
    rows_buf,
    gate_up,
    down_w,
    partial,
    opposite_in,
    merged_out,
    side_in,
    row_sum,
    opposite_in2,
    send2,
    merged_out2,
    side_in2,
    local_sem,
    send_sem,
    recv_sem,
    weight_send,
    weight_recv,
):
    right, left, upper, lower, sibling = torus_place()
    hidden = gate_ref.shape[0]
    barrier = pltpu.get_barrier_semaphore()
    for peer in (right, left, upper, lower, sibling):
        pl.semaphore_signal(barrier, inc=1, device_id=peer, device_id_type=MESH_ID)

    first = ((right, left), (upper, lower))
    second = ((upper, lower), (right, left))
    copies = []
    count = [0]

    def send(src, dst, peer):
        index = count[0]
        count[0] += 1
        copy = pltpu.make_async_remote_copy(
            src_ref=src,
            dst_ref=dst,
            send_sem=send_sem.at[index],
            recv_sem=recv_sem.at[index],
            device_id=peer,
            device_id_type=MESH_ID,
        )
        copy.start()
        copies.append(copy)
        return copy

    local = []
    sources = (gate_ref, up_ref, down_ref)
    targets = (
        gate_up.at[pl.ds(0, hidden)],
        gate_up.at[pl.ds(2 * hidden, hidden)],
        down_w.at[pl.ds(0, hidden)],
    )
    far_targets = (
        gate_up.at[pl.ds(hidden, hidden)],
        gate_up.at[pl.ds(3 * hidden, hidden)],
        down_w.at[pl.ds(hidden, hidden)],
    )
    for index, (src, dst) in enumerate(zip(sources, targets)):
        copy = pltpu.make_async_copy(src, dst, local_sem.at[index])
        copy.start()
        local.append(copy)

    def slot(group, chunk, sub, start=0, size=SUB):
        return rows_buf.at[chunk, pl.ds(group * RING * SUB + sub * SUB + start, size)]

    for group in range(2):
        rows_buf[0, pl.ds(group * RING * SUB, SUB)] = ffw_in_ref[pl.ds(group * SUB, SUB)]
    pl.semaphore_wait(barrier, 5)

    step1 = []
    for group in range(2):
        plus, minus = first[group]
        step1.append(
            (
                send(slot(group, 0, 0), slot(group, 0, 3), plus),
                send(slot(group, 0, 0), slot(group, 0, 1), minus),
            )
        )
    across = {}

    def send_across(group, sub):
        plus, minus = second[group]
        across[group, sub] = (
            send(slot(group, 0, sub), slot(group, 3, sub), plus),
            send(slot(group, 0, sub), slot(group, 1, sub), minus),
        )

    relays = {}

    def relay_across(group, sub):
        plus, minus = second[group]
        across[group, sub][0].wait_recv()
        a = send(slot(group, 3, sub, 0, HALF), slot(group, 2, sub, 0, HALF), plus)
        across[group, sub][1].wait_recv()
        b = send(slot(group, 1, sub, HALF, HALF), slot(group, 2, sub, HALF, HALF), minus)
        relays[group, sub] = (a, b)

    for group in range(2):
        send_across(group, 0)
    weight_copies = []
    for index, (src, dst) in enumerate(zip(sources, far_targets)):
        copy = pltpu.make_async_remote_copy(
            src_ref=src,
            dst_ref=dst,
            send_sem=weight_send.at[index],
            recv_sem=weight_recv.at[index],
            device_id=sibling,
            device_id_type=MESH_ID,
        )
        copy.start()
        weight_copies.append(copy)
    step2 = []
    for group in range(2):
        plus, minus = first[group]
        step1[group][0].wait_recv()
        a = send(slot(group, 0, 3, 0, HALF), slot(group, 0, 2, 0, HALF), plus)
        step1[group][1].wait_recv()
        b = send(slot(group, 0, 1, HALF, HALF), slot(group, 0, 2, HALF, HALF), minus)
        step2.append((a, b))
    for group in range(2):
        send_across(group, 1)
        send_across(group, 3)
    for group in range(2):
        relay_across(group, 0)
    for group in range(2):
        step2[group][0].wait_recv()
        step2[group][1].wait_recv()
        send_across(group, 2)

    for copy in local:
        copy.wait()
    for copy in weight_copies:
        copy.wait_recv()

    def compute(chunk):
        rows = rows_buf[chunk]
        both = lax.dot_general(
            rows, gate_up[...], (((1,), (1,)), ((), ())), preferred_element_type=jnp.float32
        )
        gate = both[:, : 2 * hidden]
        act = (jax.nn.gelu(gate, approximate=True) * both[:, 2 * hidden :]).astype(jnp.bfloat16)
        partial[chunk] = jnp.dot(act, down_w[...], preferred_element_type=jnp.float32).astype(
            jnp.bfloat16
        )

    for group in range(2):
        relay_across(group, 1)
        relay_across(group, 3)
    compute(0)
    for group in range(2):
        relay_across(group, 2)
    compute(1)

    span = RING * SUB
    half = span // 2

    def part(buf, group, chunk, which):
        return buf.at[chunk, pl.ds(group * span + which * half, half)]

    def side(group, which, low):
        return side_in.at[which, pl.ds(group * span + low * half, half)]

    plain = []
    for group in range(2):
        plus, minus = second[group]
        plain.append([send(part(partial, group, 1, 1), side(group, 0, 1), plus)])
    compute(3)
    for group in range(2):
        plus, minus = second[group]
        plain[group].append(send(part(partial, group, 3, 0), side(group, 1, 0), minus))
    for pair in relays.values():
        pair[0].wait_recv()
        pair[1].wait_recv()
    compute(2)
    opposite = []
    for group in range(2):
        plus, minus = second[group]
        opposite.append(
            (
                send(part(partial, group, 2, 0), opposite_in.at[0, pl.ds(group * half, half)], plus),
                send(part(partial, group, 2, 1), opposite_in.at[1, pl.ds(group * half, half)], minus),
            )
        )
    merged = []
    for group in range(2):
        plus, minus = second[group]
        rows = pl.ds(group * half, half)
        opposite[group][0].wait_recv()
        merged_out[0, rows] = (
            part(partial, group, 1, 0)[...].astype(jnp.float32)
            + opposite_in[0, rows].astype(jnp.float32)
        ).astype(jnp.bfloat16)
        a = send(merged_out.at[0, rows], side(group, 0, 0), plus)
        opposite[group][1].wait_recv()
        merged_out[1, rows] = (
            part(partial, group, 3, 1)[...].astype(jnp.float32)
            + opposite_in[1, rows].astype(jnp.float32)
        ).astype(jnp.bfloat16)
        b = send(merged_out.at[1, rows], side(group, 1, 1), minus)
        merged.append((a, b))

    def summed(group, sub):
        rows = pl.ds(group * span + sub * SUB, SUB)
        return (
            partial[0, rows].astype(jnp.float32)
            + side_in[0, rows].astype(jnp.float32)
            + side_in[1, rows].astype(jnp.float32)
        )

    last = []
    for group in range(2):
        plus, minus = first[group]
        plain[group][0].wait_recv()
        merged[group][1].wait_recv()
        send2[group, 2] = summed(group, 2).astype(jnp.bfloat16)
        a = send(send2.at[group, 2, pl.ds(0, HALF)], opposite_in2.at[group, 0], plus)
        b = send(send2.at[group, 2, pl.ds(HALF, HALF)], opposite_in2.at[group, 1], minus)
        last.append([a, b])
    for group in range(2):
        plus, minus = first[group]
        plain[group][1].wait_recv()
        merged[group][0].wait_recv()
        row_sum[group, 0] = summed(group, 1)
        row_sum[group, 1] = summed(group, 3)
        send2[group, 1] = row_sum[group, 0].astype(jnp.bfloat16)
        send2[group, 3] = row_sum[group, 1].astype(jnp.bfloat16)
        a = send(
            send2.at[group, 1, pl.ds(HALF, HALF)], side_in2.at[group, 0, pl.ds(HALF, HALF)], plus
        )
        b = send(send2.at[group, 3, pl.ds(0, HALF)], side_in2.at[group, 1, pl.ds(0, HALF)], minus)
        last[group] += [a, b]
    for group in range(2):
        plus, minus = first[group]
        last[group][0].wait_recv()
        merged_out2[group, 0] = (
            row_sum[group, 0, pl.ds(0, HALF)] + opposite_in2[group, 0].astype(jnp.float32)
        ).astype(jnp.bfloat16)
        a = send(merged_out2.at[group, 0], side_in2.at[group, 0, pl.ds(0, HALF)], plus)
        last[group][1].wait_recv()
        merged_out2[group, 1] = (
            row_sum[group, 1, pl.ds(HALF, HALF)] + opposite_in2[group, 1].astype(jnp.float32)
        ).astype(jnp.bfloat16)
        b = send(merged_out2.at[group, 1], side_in2.at[group, 1, pl.ds(HALF, HALF)], minus)
        last[group] += [a, b]
    for group in range(2):
        own = summed(group, 0)
        for index in (2, 3, 4, 5):
            last[group][index].wait_recv()
        total = own + side_in2[group, 0].astype(jnp.float32) + side_in2[group, 1].astype(jnp.float32)
        rows = pl.ds(group * SUB, SUB)
        out_ref[rows] = (residual_ref[rows] + normed(total, gain_ref[...])).astype(out_ref.dtype)

    for copy in copies:
        copy.wait_send()
    for copy in weight_copies:
        copy.wait_send()


def ffn_block(ffw_in, residual, gain, gate_t, up_t, down_weight):
    rows, width = ffw_in.shape
    hidden = gate_t.shape[0]
    vmem = pl.BlockSpec(memory_space=pltpu.VMEM)
    hbm = pl.BlockSpec(memory_space=pl.ANY)
    bf16 = jnp.bfloat16
    span = RING * SUB
    copies = 64
    return pl.pallas_call(
        ffn_kernel,
        out_shape=jax.ShapeDtypeStruct((rows, width), bf16),
        in_specs=[vmem, vmem, vmem, hbm, hbm, hbm],
        out_specs=vmem,
        scratch_shapes=[
            pltpu.VMEM((RING, 2 * span, width), bf16),
            pltpu.VMEM((4 * hidden, width), bf16),
            pltpu.VMEM((2 * hidden, width), bf16),
            pltpu.VMEM((RING, 2 * span, width), bf16),
            pltpu.VMEM((2, span, width), bf16),
            pltpu.VMEM((2, span, width), bf16),
            pltpu.VMEM((2, 2 * span, width), bf16),
            pltpu.VMEM((2, 2, SUB, width), jnp.float32),
            pltpu.VMEM((2, 2, HALF, width), bf16),
            pltpu.VMEM((2, RING, SUB, width), bf16),
            pltpu.VMEM((2, 2, HALF, width), bf16),
            pltpu.VMEM((2, 2, SUB, width), bf16),
            pltpu.SemaphoreType.DMA((3,)),
            pltpu.SemaphoreType.DMA((copies,)),
            pltpu.SemaphoreType.DMA((copies,)),
            pltpu.SemaphoreType.DMA((3,)),
            pltpu.SemaphoreType.DMA((3,)),
        ],
        compiler_params=pltpu.CompilerParams(
            collective_id=0, has_side_effects=True, vmem_limit_bytes=58 << 20
        ),
        name="ffn_block",
    )(ffw_in, residual, gain, gate_t, up_t, down_weight)


def body(
    states,
    attn_gain,
    query_matrix,
    key_matrix,
    value_matrix,
    query_gain,
    key_gain,
    out_weight,
    post_gain,
    ffw_gain,
    gate_weight,
    up_weight,
    down_weight,
    post_ffw_gain,
    prefix_key_cache,
    prefix_value_cache,
    segment,
    prefix_id,
    owner_map,
):
    row_count = states.shape[0]
    head_dim = query_gain.shape[0]
    kv_heads = key_matrix.shape[1] // head_dim
    head_cols = query_matrix.shape[1]
    query_group_width = head_cols // (kv_heads * head_dim)
    score_scale = head_dim ** (-0.5)
    req_count = lax.axis_size("req")
    mlp_count = lax.axis_size("mlp")
    mlp_index = lax.axis_index("mlp")
    quarter = row_count // mlp_count
    states_f = states.astype(jnp.float32)
    normalized_input = normed(states_f, attn_gain).astype(jnp.bfloat16)
    unnormed_queries = jnp.dot(
        normalized_input, query_matrix, preferred_element_type=jnp.float32
    ).reshape(row_count, kv_heads, query_group_width, head_dim)
    query_vectors = normed(unnormed_queries, query_gain).astype(jnp.bfloat16)
    unnormed_keys = jnp.dot(
        normalized_input, key_matrix, preferred_element_type=jnp.float32
    ).reshape(row_count, kv_heads, head_dim)
    key_vectors = normed(unnormed_keys, key_gain).astype(jnp.bfloat16)
    value_vectors = (
        jnp.dot(normalized_input, value_matrix, preferred_element_type=jnp.float32)
        .astype(jnp.bfloat16)
        .reshape(row_count, kv_heads, head_dim)
    )
    prefix_count = owner_map.shape[0]
    prefix_onehot = (
        prefix_id[:, None] == jnp.arange(prefix_count, dtype=jnp.int32)[None, :]
    ).astype(jnp.int32)
    target = jnp.sum(prefix_onehot * owner_map[None, :], axis=1)
    to_owner = (target[:, None] == jnp.arange(req_count, dtype=jnp.int32)[None, :]).astype(
        jnp.float32
    )
    token_position = jnp.arange(row_count, dtype=jnp.int32)
    earlier = (token_position[:, None] > token_position[None, :]).astype(jnp.float32)
    counts = jnp.dot(earlier, to_owner, precision=lax.Precision.HIGHEST)
    slot_index = jnp.sum(to_owner * counts, axis=1).astype(jnp.int32)
    place_row = target * CAP + slot_index
    placing = (place_row[None, :] == jnp.arange(req_count * CAP, dtype=jnp.int32)[:, None]).astype(
        jnp.bfloat16
    )
    outgoing = (
        jnp.dot(
            placing, query_vectors.reshape(row_count, head_cols), preferred_element_type=jnp.float32
        )
        .astype(jnp.bfloat16)
        .reshape(req_count, CAP, head_cols)
    )
    stored_keys = prefix_key_cache[0].reshape(-1, kv_heads, head_dim)
    stored_values = prefix_value_cache[0].reshape(-1, kv_heads, head_dim)
    suffix_output, suffix_log_sum = local_attention(
        query_vectors, key_vectors, value_vectors, segment, score_scale
    )
    mixed, log_total = prefix_partials(
        lax.all_to_all(outgoing, "req", split_axis=0, concat_axis=0, tiled=True),
        stored_keys,
        stored_values,
        score_scale,
    )
    back_out = lax.all_to_all(
        mixed.astype(jnp.bfloat16), "req", split_axis=0, concat_axis=0, tiled=True
    ).astype(mixed.dtype)
    back_lse = lax.all_to_all(
        log_total.astype(jnp.bfloat16), "req", split_axis=0, concat_axis=0, tiled=True
    ).astype(log_total.dtype)
    prefix_out = back_out.reshape(req_count * CAP, head_cols)[place_row].reshape(
        row_count, kv_heads, query_group_width, head_dim
    )
    prefix_lse = back_lse.reshape(req_count * CAP, kv_heads * query_group_width)[place_row].reshape(
        row_count, kv_heads, query_group_width
    )
    prefix_out, prefix_lse = (prefix_out, prefix_lse)
    blend = jax.nn.sigmoid(prefix_lse - suffix_log_sum)[..., None]
    attended = (
        (blend * prefix_out + (1.0 - blend) * suffix_output)
        .astype(jnp.bfloat16)
        .reshape(row_count, head_cols)
    )
    partial_value = jnp.dot(attended, out_weight, preferred_element_type=jnp.float32)
    full_sum = lax.psum(partial_value.astype(jnp.bfloat16), "mlp").astype(jnp.float32)
    summed = lax.dynamic_slice_in_dim(full_sum, mlp_index * quarter, quarter, 0)
    own_rows = lax.dynamic_slice_in_dim(states_f, mlp_index * quarter, quarter, 0)
    residual = own_rows + normed(summed, post_gain)
    ffw_in = normed(residual, ffw_gain).astype(jnp.bfloat16)
    return ffn_block(
        ffw_in, residual, post_ffw_gain[None], gate_weight.T, up_weight.T, down_weight
    )


def solution(mesh):
    return jax.shard_map(
        body,
        mesh=mesh,
        in_specs=(
            P("req", None),
            P(),
            P(None, "mlp"),
            P(None, "mlp"),
            P(None, "mlp"),
            P(),
            P(),
            P("mlp", None),
            P(),
            P(),
            P(None, "req"),
            P(None, "req"),
            P("req", None),
            P(),
            P("req", None, "mlp"),
            P("req", None, "mlp"),
            P("req"),
            P("req"),
            P(),
        ),
        out_specs=P(("req", "mlp"), None),
        check_vma=False,
    )
```

```python
import jax
import jax.numpy as jnp
from jax import lax
from jax.experimental import pallas as pl
from jax.experimental.pallas import tpu as pltpu
from jax.sharding import PartitionSpec as P

CAP = 32


EPS = 1e-06


def normed(values_in, gain_vec):
    return (
        values_in
        * lax.rsqrt(jnp.mean(values_in * values_in, axis=-1, keepdims=True) + EPS)
        * gain_vec
    )


MESH_ID = pl.DeviceIdType.MESH
RING = 4
SUB = 32
HALF = 16


def torus_place():
    me = lax.axis_index("req")
    layer = lax.axis_index("mlp")
    core = lax.rem(me, 2)
    chip = me // 2
    col = lax.rem(chip, RING)
    row = chip // RING

    def at(row_at, col_at, core_at):
        return ((row_at * RING + col_at) * 2 + core_at, layer)

    up = at(lax.rem(row + 1, RING), col, core)
    down = at(lax.rem(row + RING - 1, RING), col, core)
    right = at(row, lax.rem(col + 1, RING), core)
    left = at(row, lax.rem(col + RING - 1, RING), core)
    sibling = at(row, col, 1 - core)
    return right, left, up, down, sibling


def ffn_kernel(
    ffw_in_ref,
    residual_ref,
    gain_ref,
    gate_ref,
    up_ref,
    down_ref,
    out_ref,
    rows_buf,
    gate_up,
    down_w,
    partial,
    opposite_in,
    merged_out,
    side_in,
    row_sum,
    opposite_in2,
    send2,
    merged_out2,
    side_in2,
    local_sem,
    send_sem,
    recv_sem,
    weight_send,
    weight_recv,
):
    right, left, upper, lower, sibling = torus_place()
    hidden = gate_ref.shape[0]
    barrier = pltpu.get_barrier_semaphore()
    for peer in (right, left, upper, lower, sibling):
        pl.semaphore_signal(barrier, inc=1, device_id=peer, device_id_type=MESH_ID)

    first = ((right, left), (upper, lower))
    second = ((upper, lower), (right, left))
    copies = []
    count = [0]

    def send(src, dst, peer):
        index = count[0]
        count[0] += 1
        copy = pltpu.make_async_remote_copy(
            src_ref=src,
            dst_ref=dst,
            send_sem=send_sem.at[index],
            recv_sem=recv_sem.at[index],
            device_id=peer,
            device_id_type=MESH_ID,
        )
        copy.start()
        copies.append(copy)
        return copy

    local = []
    sources = (gate_ref, up_ref, down_ref)
    targets = (
        gate_up.at[pl.ds(0, hidden)],
        gate_up.at[pl.ds(2 * hidden, hidden)],
        down_w.at[pl.ds(0, hidden)],
    )
    far_targets = (
        gate_up.at[pl.ds(hidden, hidden)],
        gate_up.at[pl.ds(3 * hidden, hidden)],
        down_w.at[pl.ds(hidden, hidden)],
    )
    for index, (src, dst) in enumerate(zip(sources, targets)):
        copy = pltpu.make_async_copy(src, dst, local_sem.at[index])
        copy.start()
        local.append(copy)

    def slot(group, chunk, sub, start=0, size=SUB):
        return rows_buf.at[chunk, pl.ds(group * RING * SUB + sub * SUB + start, size)]

    for group in range(2):
        rows_buf[0, pl.ds(group * RING * SUB, SUB)] = ffw_in_ref[pl.ds(group * SUB, SUB)]
    pl.semaphore_wait(barrier, 5)

    step1 = []
    for group in range(2):
        plus, minus = first[group]
        step1.append(
            (
                send(slot(group, 0, 0), slot(group, 0, 3), plus),
                send(slot(group, 0, 0), slot(group, 0, 1), minus),
            )
        )
    across = {}

    def send_across(group, sub):
        plus, minus = second[group]
        across[group, sub] = (
            send(slot(group, 0, sub), slot(group, 3, sub), plus),
            send(slot(group, 0, sub), slot(group, 1, sub), minus),
        )

    relays = {}

    def relay_across(group, sub):
        plus, minus = second[group]
        across[group, sub][0].wait_recv()
        a = send(slot(group, 3, sub, 0, HALF), slot(group, 2, sub, 0, HALF), plus)
        across[group, sub][1].wait_recv()
        b = send(slot(group, 1, sub, HALF, HALF), slot(group, 2, sub, HALF, HALF), minus)
        relays[group, sub] = (a, b)

    for group in range(2):
        send_across(group, 0)
    weight_copies = []
    for index, (src, dst) in enumerate(zip(sources, far_targets)):
        copy = pltpu.make_async_remote_copy(
            src_ref=src,
            dst_ref=dst,
            send_sem=weight_send.at[index],
            recv_sem=weight_recv.at[index],
            device_id=sibling,
            device_id_type=MESH_ID,
        )
        copy.start()
        weight_copies.append(copy)
    step2 = []
    for group in range(2):
        plus, minus = first[group]
        step1[group][0].wait_recv()
        a = send(slot(group, 0, 3, 0, HALF), slot(group, 0, 2, 0, HALF), plus)
        step1[group][1].wait_recv()
        b = send(slot(group, 0, 1, HALF, HALF), slot(group, 0, 2, HALF, HALF), minus)
        step2.append((a, b))
    for group in range(2):
        send_across(group, 1)
        send_across(group, 3)
    for group in range(2):
        relay_across(group, 0)
    for group in range(2):
        step2[group][0].wait_recv()
        step2[group][1].wait_recv()
        send_across(group, 2)

    for copy in local:
        copy.wait()
    for copy in weight_copies:
        copy.wait_recv()

    def compute(chunk):
        rows = rows_buf[chunk]
        both = lax.dot_general(
            rows, gate_up[...], (((1,), (1,)), ((), ())), preferred_element_type=jnp.float32
        )
        gate = both[:, : 2 * hidden]
        act = (jax.nn.gelu(gate, approximate=True) * both[:, 2 * hidden :]).astype(jnp.bfloat16)
        partial[chunk] = jnp.dot(act, down_w[...], preferred_element_type=jnp.float32).astype(
            jnp.bfloat16
        )

    for group in range(2):
        relay_across(group, 1)
        relay_across(group, 3)
    compute(0)
    for group in range(2):
        relay_across(group, 2)
    compute(1)

    span = RING * SUB
    half = span // 2

    def part(buf, group, chunk, which):
        return buf.at[chunk, pl.ds(group * span + which * half, half)]

    def side(group, which, low):
        return side_in.at[which, pl.ds(group * span + low * half, half)]

    plain = []
    for group in range(2):
        plus, minus = second[group]
        plain.append([send(part(partial, group, 1, 1), side(group, 0, 1), plus)])
    compute(3)
    for group in range(2):
        plus, minus = second[group]
        plain[group].append(send(part(partial, group, 3, 0), side(group, 1, 0), minus))
    for pair in relays.values():
        pair[0].wait_recv()
        pair[1].wait_recv()
    compute(2)
    opposite = []
    for group in range(2):
        plus, minus = second[group]
        opposite.append(
            (
                send(part(partial, group, 2, 0), opposite_in.at[0, pl.ds(group * half, half)], plus),
                send(part(partial, group, 2, 1), opposite_in.at[1, pl.ds(group * half, half)], minus),
            )
        )
    merged = []
    for group in range(2):
        plus, minus = second[group]
        rows = pl.ds(group * half, half)
        opposite[group][0].wait_recv()
        merged_out[0, rows] = (
            part(partial, group, 1, 0)[...].astype(jnp.float32)
            + opposite_in[0, rows].astype(jnp.float32)
        ).astype(jnp.bfloat16)
        a = send(merged_out.at[0, rows], side(group, 0, 0), plus)
        opposite[group][1].wait_recv()
        merged_out[1, rows] = (
            part(partial, group, 3, 1)[...].astype(jnp.float32)
            + opposite_in[1, rows].astype(jnp.float32)
        ).astype(jnp.bfloat16)
        b = send(merged_out.at[1, rows], side(group, 1, 1), minus)
        merged.append((a, b))

    def summed(group, sub):
        rows = pl.ds(group * span + sub * SUB, SUB)
        return (
            partial[0, rows].astype(jnp.float32)
            + side_in[0, rows].astype(jnp.float32)
            + side_in[1, rows].astype(jnp.float32)
        )

    last = []
    for group in range(2):
        plus, minus = first[group]
        plain[group][0].wait_recv()
        merged[group][1].wait_recv()
        send2[group, 2] = summed(group, 2).astype(jnp.bfloat16)
        a = send(send2.at[group, 2, pl.ds(0, HALF)], opposite_in2.at[group, 0], plus)
        b = send(send2.at[group, 2, pl.ds(HALF, HALF)], opposite_in2.at[group, 1], minus)
        last.append([a, b])
    for group in range(2):
        plus, minus = first[group]
        plain[group][1].wait_recv()
        merged[group][0].wait_recv()
        row_sum[group, 0] = summed(group, 1)
        row_sum[group, 1] = summed(group, 3)
        send2[group, 1] = row_sum[group, 0].astype(jnp.bfloat16)
        send2[group, 3] = row_sum[group, 1].astype(jnp.bfloat16)
        a = send(
            send2.at[group, 1, pl.ds(HALF, HALF)], side_in2.at[group, 0, pl.ds(HALF, HALF)], plus
        )
        b = send(send2.at[group, 3, pl.ds(0, HALF)], side_in2.at[group, 1, pl.ds(0, HALF)], minus)
        last[group] += [a, b]
    for group in range(2):
        plus, minus = first[group]
        last[group][0].wait_recv()
        merged_out2[group, 0] = (
            row_sum[group, 0, pl.ds(0, HALF)] + opposite_in2[group, 0].astype(jnp.float32)
        ).astype(jnp.bfloat16)
        a = send(merged_out2.at[group, 0], side_in2.at[group, 0, pl.ds(0, HALF)], plus)
        last[group][1].wait_recv()
        merged_out2[group, 1] = (
            row_sum[group, 1, pl.ds(HALF, HALF)] + opposite_in2[group, 1].astype(jnp.float32)
        ).astype(jnp.bfloat16)
        b = send(merged_out2.at[group, 1], side_in2.at[group, 1, pl.ds(HALF, HALF)], minus)
        last[group] += [a, b]
    for group in range(2):
        own = summed(group, 0)
        for index in (2, 3, 4, 5):
            last[group][index].wait_recv()
        total = own + side_in2[group, 0].astype(jnp.float32) + side_in2[group, 1].astype(jnp.float32)
        rows = pl.ds(group * SUB, SUB)
        out_ref[rows] = (residual_ref[rows] + normed(total, gain_ref[...])).astype(out_ref.dtype)

    for copy in copies:
        copy.wait_send()
    for copy in weight_copies:
        copy.wait_send()


def ffn_block(ffw_in, residual, gain, gate_t, up_t, down_weight):
    rows, width = ffw_in.shape
    hidden = gate_t.shape[0]
    vmem = pl.BlockSpec(memory_space=pltpu.VMEM)
    hbm = pl.BlockSpec(memory_space=pl.ANY)
    bf16 = jnp.bfloat16
    span = RING * SUB
    copies = 64
    return pl.pallas_call(
        ffn_kernel,
        out_shape=jax.ShapeDtypeStruct((rows, width), bf16),
        in_specs=[vmem, vmem, vmem, hbm, hbm, hbm],
        out_specs=vmem,
        scratch_shapes=[
            pltpu.VMEM((RING, 2 * span, width), bf16),
            pltpu.VMEM((4 * hidden, width), bf16),
            pltpu.VMEM((2 * hidden, width), bf16),
            pltpu.VMEM((RING, 2 * span, width), bf16),
            pltpu.VMEM((2, span, width), bf16),
            pltpu.VMEM((2, span, width), bf16),
            pltpu.VMEM((2, 2 * span, width), bf16),
            pltpu.VMEM((2, 2, SUB, width), jnp.float32),
            pltpu.VMEM((2, 2, HALF, width), bf16),
            pltpu.VMEM((2, RING, SUB, width), bf16),
            pltpu.VMEM((2, 2, HALF, width), bf16),
            pltpu.VMEM((2, 2, SUB, width), bf16),
            pltpu.SemaphoreType.DMA((3,)),
            pltpu.SemaphoreType.DMA((copies,)),
            pltpu.SemaphoreType.DMA((copies,)),
            pltpu.SemaphoreType.DMA((3,)),
            pltpu.SemaphoreType.DMA((3,)),
        ],
        compiler_params=pltpu.CompilerParams(
            collective_id=0, has_side_effects=True, vmem_limit_bytes=58 << 20
        ),
        name="ffn_block",
    )(ffw_in, residual, gain, gate_t, up_t, down_weight)


def plane_place():
    me = lax.axis_index("req")
    layer = lax.axis_index("mlp")
    core = lax.rem(me, 2)
    chip = me // 2
    return chip // RING, lax.rem(chip, RING), core, layer


def attention_kernel(
    states_ref,
    attn_gain_ref,
    query_gain_ref,
    key_gain_ref,
    segment_ref,
    prefix_ref,
    owner_ref,
    query_w_ref,
    key_w_ref,
    value_w_ref,
    keys_ref,
    values_ref,
    out_ref,
    query_w,
    key_w,
    value_w,
    stored_keys,
    stored_values,
    outgoing,
    incoming,
    results,
    back,
    local_sem,
    send_sem,
    recv_sem,
    back_send_sem,
    back_recv_sem,
):
    row, col, core, layer = plane_place()
    rows, width = states_ref.shape
    head = query_gain_ref.shape[1]
    heads = query_w.shape[1] // head
    peers = 2 * RING * RING
    score_scale = head ** (-0.5)
    f32, bf16 = jnp.float32, jnp.bfloat16

    def shifted(offset, sign):
        down, across, flip = offset // (2 * RING), (offset // 2) % RING, offset % 2
        if sign < 0:
            down, across = (RING - down) % RING, (RING - across) % RING
        row_at = lax.rem(row + down, RING)
        col_at = lax.rem(col + across, RING)
        core_at = 1 - core if flip else core
        return ((row_at * RING + col_at) * 2 + core_at, layer)

    barrier = pltpu.get_barrier_semaphore()
    for offset in range(1, peers):
        pl.semaphore_signal(barrier, inc=1, device_id=shifted(offset, 1), device_id_type=MESH_ID)
    local = []
    for index, (src, dst) in enumerate(
        (
            (query_w_ref, query_w),
            (key_w_ref, key_w),
            (value_w_ref, value_w),
            (keys_ref, stored_keys),
            (values_ref, stored_values),
        )
    ):
        copy = pltpu.make_async_copy(src, dst, local_sem.at[index])
        copy.start()
        local.append(copy)

    normalized = normed(states_ref[...].astype(f32), attn_gain_ref[...]).astype(bf16)

    def column(line):
        return jnp.transpose(jnp.broadcast_to(line, (128, rows)))[:, :1]

    prefix_row = prefix_ref[...].astype(f32)
    prefix_col = column(prefix_row)
    row_at = lax.broadcasted_iota(jnp.int32, (rows, rows), 0)
    col_at = lax.broadcasted_iota(jnp.int32, (rows, rows), 1)
    same = jnp.where(prefix_col == prefix_row, 1.0, 0.0)
    rank_col = jnp.sum(jnp.where(col_at < row_at, same, 0.0), axis=1, keepdims=True)
    rank_row = jnp.sum(jnp.where(row_at < col_at, same, 0.0), axis=0, keepdims=True)
    groups = owner_ref.shape[1]
    onehot = prefix_col == lax.broadcasted_iota(jnp.int32, (rows, groups), 1).astype(f32)
    owner_col = jnp.sum(jnp.where(onehot, owner_ref[...].astype(f32), 0.0), axis=1, keepdims=True)
    owner_row = jnp.transpose(jnp.broadcast_to(owner_col, (rows, 128)))[:1]

    def place(owner, rank):
        owner = owner.astype(jnp.int32)
        down = ((owner >> 3) - row) & 3
        across = (((owner >> 1) & 3) - col) & 3
        flip = ((owner & 1) - core) & 1
        return (down * 8 + across * 2 + flip) * CAP + rank.astype(jnp.int32)

    place_col = place(owner_col, rank_col)
    place_row = place(owner_row, rank_row)

    local[0].wait()
    raw = jnp.dot(normalized, query_w[...], preferred_element_type=f32)
    queries = [
        normed(raw[:, g * head : (g + 1) * head], query_gain_ref[...]).astype(bf16)
        for g in range(heads)
    ]
    query_rows = jnp.concatenate(queries, axis=1)
    pl.semaphore_wait(barrier, peers - 1)
    sends = {}
    batch = 2 * RING
    for part in range(peers // batch):
        slots = lax.broadcasted_iota(jnp.int32, (batch * CAP, rows), 0) + part * batch * CAP
        placing = jnp.where(slots == place_row, 1.0, 0.0).astype(bf16)
        packed = jnp.dot(placing, query_rows, preferred_element_type=f32).astype(bf16)
        packed = packed.reshape(batch, CAP, heads * head)
        if part == 0:
            incoming[0] = packed[0]
        outgoing[pl.ds(part * batch, batch)] = packed
        for offset in range(max(part * batch, 1), (part + 1) * batch):
            copy = pltpu.make_async_remote_copy(
                src_ref=outgoing.at[offset],
                dst_ref=incoming.at[offset],
                send_sem=send_sem.at[offset],
                recv_sem=recv_sem.at[offset],
                device_id=shifted(offset, 1),
                device_id_type=MESH_ID,
            )
            copy.start()
            sends[offset] = copy

    local[1].wait()
    local[2].wait()
    raw = jnp.dot(normalized, key_w[...], preferred_element_type=f32)
    keys = normed(raw, key_gain_ref[...]).astype(bf16)
    values = jnp.dot(normalized, value_w[...], preferred_element_type=f32).astype(bf16)
    segment_row = segment_ref[...].astype(f32)
    allowed = (column(segment_row) == segment_row) & (row_at >= col_at)

    def attend(query, key, value, mask):
        scores = (
            lax.dot_general(query, key, (((1,), (1,)), ((), ())), preferred_element_type=f32)
            * score_scale
        )
        if mask is not None:
            scores = jnp.where(mask, scores, -jnp.inf)
        row_max = jnp.max(scores, axis=-1, keepdims=True)
        powers = jnp.exp(scores - row_max)
        total = jnp.sum(powers, axis=-1, keepdims=True)
        weights = (powers / total).astype(bf16)
        mixed = jnp.dot(weights, value, preferred_element_type=f32)
        return mixed, row_max + jnp.log(total)

    suffix = [attend(query, keys, values, allowed) for query in queries]

    local[3].wait()
    local[4].wait()
    lanes = lax.broadcasted_iota(jnp.int32, (batch * CAP, 128), 1)
    returns = {}
    for part in range(peers // batch):
        for offset in range(max(part * batch, 1), (part + 1) * batch):
            sends[offset].wait_recv()
        query = incoming[pl.ds(part * batch, batch)].reshape(batch * CAP, heads * head)
        tail = jnp.zeros((batch * CAP, 128), f32)
        for g in range(heads):
            mixed, log_total = attend(
                query[:, g * head : (g + 1) * head], stored_keys[...], stored_values[...], None
            )
            coarse = log_total.astype(bf16).astype(f32)
            tail = jnp.where(lanes == 2 * g, coarse, tail)
            tail = jnp.where(lanes == 2 * g + 1, log_total - coarse, tail)
            results[pl.ds(part * batch, batch), :, pl.ds(g * head, head)] = mixed.astype(
                bf16
            ).reshape(batch, CAP, head)
        results[pl.ds(part * batch, batch), :, pl.ds(heads * head, 128)] = tail.astype(
            bf16
        ).reshape(batch, CAP, 128)
        if part == 0:
            back[0] = results[0]
        for offset in range(max(part * batch, 1), (part + 1) * batch):
            copy = pltpu.make_async_remote_copy(
                src_ref=results.at[offset],
                dst_ref=back.at[offset],
                send_sem=back_send_sem.at[offset],
                recv_sem=back_recv_sem.at[offset],
                device_id=shifted(offset, -1),
                device_id_type=MESH_ID,
            )
            copy.start()
            returns[offset] = copy

    picked = jnp.zeros((rows, heads * head + 128), f32)
    for part in range(peers // batch):
        for offset in range(max(part * batch, 1), (part + 1) * batch):
            returns[offset].wait_recv()
        slots = lax.broadcasted_iota(jnp.int32, (rows, batch * CAP), 1) + part * batch * CAP
        choosing = jnp.where(slots == place_col, 1.0, 0.0).astype(bf16)
        block = back[pl.ds(part * batch, batch)].reshape(batch * CAP, heads * head + 128)
        picked = picked + jnp.dot(choosing, block, preferred_element_type=f32)
    for g in range(heads):
        mixed, log_total = suffix[g]
        at = heads * head + 2 * g
        prefix_lse = picked[:, at : at + 1] + picked[:, at + 1 : at + 2]
        blend = jax.nn.sigmoid(prefix_lse - log_total)
        columns = slice(g * head, (g + 1) * head)
        out_ref[:, columns] = (blend * picked[:, columns] + (1.0 - blend) * mixed).astype(bf16)

    for offset in range(1, peers):
        sends[offset].wait_send()
        returns[offset].wait_send()


def attention_block(
    states, attn_gain, query_gain, key_gain, segment, prefix_id, owner_map, query_w, key_w, value_w, keys, values
):
    rows, width = states.shape
    vmem = pl.BlockSpec(memory_space=pltpu.VMEM)
    hbm = pl.BlockSpec(memory_space=pl.ANY)
    bf16 = jnp.bfloat16
    peers = 2 * RING * RING
    cols = query_w.shape[1]
    return pl.pallas_call(
        attention_kernel,
        out_shape=jax.ShapeDtypeStruct((rows, cols), bf16),
        in_specs=[vmem] * 7 + [hbm] * 5,
        out_specs=vmem,
        scratch_shapes=[
            pltpu.VMEM(query_w.shape, bf16),
            pltpu.VMEM(key_w.shape, bf16),
            pltpu.VMEM(value_w.shape, bf16),
            pltpu.VMEM(keys.shape, bf16),
            pltpu.VMEM(values.shape, bf16),
            pltpu.VMEM((peers, CAP, cols), bf16),
            pltpu.VMEM((peers, CAP, cols), bf16),
            pltpu.VMEM((peers, CAP, cols + 128), bf16),
            pltpu.VMEM((peers, CAP, cols + 128), bf16),
            pltpu.SemaphoreType.DMA((5,)),
            pltpu.SemaphoreType.DMA((peers,)),
            pltpu.SemaphoreType.DMA((peers,)),
            pltpu.SemaphoreType.DMA((peers,)),
            pltpu.SemaphoreType.DMA((peers,)),
        ],
        compiler_params=pltpu.CompilerParams(
            collective_id=1, has_side_effects=True, vmem_limit_bytes=58 << 20
        ),
        name="attention_block",
    )(
        states,
        attn_gain,
        query_gain,
        key_gain,
        segment,
        prefix_id,
        owner_map,
        query_w,
        key_w,
        value_w,
        keys,
        values,
    )


def body(
    states,
    attn_gain,
    query_matrix,
    key_matrix,
    value_matrix,
    query_gain,
    key_gain,
    out_weight,
    post_gain,
    ffw_gain,
    gate_weight,
    up_weight,
    down_weight,
    post_ffw_gain,
    prefix_key_cache,
    prefix_value_cache,
    segment,
    prefix_id,
    owner_map,
):
    mlp_count = lax.axis_size("mlp")
    mlp_index = lax.axis_index("mlp")
    quarter = states.shape[0] // mlp_count
    states_f = states.astype(jnp.float32)
    attended = attention_block(
        states,
        attn_gain[None],
        query_gain[None],
        key_gain[None],
        segment[None],
        prefix_id[None],
        owner_map[None],
        query_matrix,
        key_matrix,
        value_matrix,
        prefix_key_cache[0],
        prefix_value_cache[0],
    )
    partial_value = jnp.dot(attended, out_weight, preferred_element_type=jnp.float32)
    full_sum = lax.psum(partial_value.astype(jnp.bfloat16), "mlp").astype(jnp.float32)
    summed = lax.dynamic_slice_in_dim(full_sum, mlp_index * quarter, quarter, 0)
    own_rows = lax.dynamic_slice_in_dim(states_f, mlp_index * quarter, quarter, 0)
    residual = own_rows + normed(summed, post_gain)
    ffw_in = normed(residual, ffw_gain).astype(jnp.bfloat16)
    return ffn_block(
        ffw_in, residual, post_ffw_gain[None], gate_weight.T, up_weight.T, down_weight
    )


def solution(mesh):
    return jax.shard_map(
        body,
        mesh=mesh,
        in_specs=(
            P("req", None),
            P(),
            P(None, "mlp"),
            P(None, "mlp"),
            P(None, "mlp"),
            P(),
            P(),
            P("mlp", None),
            P(),
            P(),
            P(None, "req"),
            P(None, "req"),
            P("req", None),
            P(),
            P("req", None, "mlp"),
            P("req", None, "mlp"),
            P("req"),
            P("req"),
            P(),
        ),
        out_specs=P(("req", "mlp"), None),
        check_vma=False,
    )
```

```python
import jax
import jax.numpy as jnp
from jax import lax
from jax.experimental import pallas as pl
from jax.experimental.pallas import tpu as pltpu
from jax.sharding import PartitionSpec as P

CAP = 32


EPS = 1e-06


def normed(values_in, gain_vec):
    return (
        values_in
        * lax.rsqrt(jnp.mean(values_in * values_in, axis=-1, keepdims=True) + EPS)
        * gain_vec
    )


MESH_ID = pl.DeviceIdType.MESH
RING = 4
SUB = 32
HALF = 16


def torus_place():
    me = lax.axis_index("req")
    layer = lax.axis_index("mlp")
    core = lax.rem(me, 2)
    chip = me // 2
    col = lax.rem(chip, RING)
    row = chip // RING

    def at(row_at, col_at, core_at):
        return ((row_at * RING + col_at) * 2 + core_at, layer)

    up = at(lax.rem(row + 1, RING), col, core)
    down = at(lax.rem(row + RING - 1, RING), col, core)
    right = at(row, lax.rem(col + 1, RING), core)
    left = at(row, lax.rem(col + RING - 1, RING), core)
    sibling = at(row, col, 1 - core)
    above = (me, lax.rem(layer + 1, RING))
    below = (me, lax.rem(layer + RING - 1, RING))
    return right, left, up, down, sibling, above, below


def ffn_kernel(
    attended_ref,
    post_gain_ref,
    ffw_gain_ref,
    gain_ref,
    states_ref,
    out_w_ref,
    gate_ref,
    up_ref,
    down_ref,
    out_ref,
    out_w,
    own_states,
    layer_out,
    layer_opposite,
    layer_merged,
    layer_side,
    residual,
    rows_buf,
    gate_up,
    down_w,
    partial,
    opposite_in,
    merged_out,
    side_in,
    row_sum,
    opposite_in2,
    send2,
    merged_out2,
    side_in2,
    local_sem,
    send_sem,
    recv_sem,
    weight_send,
    weight_recv,
):
    right, left, upper, lower, sibling, above, below = torus_place()
    layer = lax.axis_index("mlp")
    quarter = 2 * SUB
    f32, bf16 = jnp.float32, jnp.bfloat16
    hidden = gate_ref.shape[0]
    barrier = pltpu.get_barrier_semaphore()
    neighbours = (right, left, upper, lower, sibling, above, below)
    for peer in neighbours:
        pl.semaphore_signal(barrier, inc=1, device_id=peer, device_id_type=MESH_ID)

    first = ((right, left), (upper, lower))
    second = ((upper, lower), (right, left))
    copies = []
    count = [0]

    def send(src, dst, peer):
        index = count[0]
        count[0] += 1
        copy = pltpu.make_async_remote_copy(
            src_ref=src,
            dst_ref=dst,
            send_sem=send_sem.at[index],
            recv_sem=recv_sem.at[index],
            device_id=peer,
            device_id_type=MESH_ID,
        )
        copy.start()
        copies.append(copy)
        return copy

    layer_copies = []
    for index, (src, dst) in enumerate(
        ((out_w_ref, out_w), (states_ref.at[pl.ds(layer * quarter, quarter)], own_states))
    ):
        copy = pltpu.make_async_copy(src, dst, local_sem.at[3 + index])
        copy.start()
        layer_copies.append(copy)
    local = []
    sources = (gate_ref, up_ref, down_ref)
    targets = (
        gate_up.at[pl.ds(0, hidden)],
        gate_up.at[pl.ds(2 * hidden, hidden)],
        down_w.at[pl.ds(0, hidden)],
    )
    far_targets = (
        gate_up.at[pl.ds(hidden, hidden)],
        gate_up.at[pl.ds(3 * hidden, hidden)],
        down_w.at[pl.ds(hidden, hidden)],
    )
    for index, (src, dst) in enumerate(zip(sources, targets)):
        copy = pltpu.make_async_copy(src, dst, local_sem.at[index])
        copy.start()
        local.append(copy)

    def slot(group, chunk, sub, start=0, size=SUB):
        return rows_buf.at[chunk, pl.ds(group * RING * SUB + sub * SUB + start, size)]

    for copy in layer_copies:
        copy.wait()

    def projected(offset):
        rows = pl.ds(lax.rem(layer + offset, RING) * quarter, quarter)
        return jnp.dot(attended_ref[rows], out_w[...], preferred_element_type=f32)

    layer_out[2] = projected(2).astype(bf16)
    pl.semaphore_wait(barrier, len(neighbours))
    layer_opp = []
    for group in range(2):
        layer_opp.append(
            (
                send(
                    layer_out.at[2, pl.ds(group * SUB, HALF)], layer_opposite.at[0, group], above
                ),
                send(
                    layer_out.at[2, pl.ds(group * SUB + HALF, HALF)],
                    layer_opposite.at[1, group],
                    below,
                ),
            )
        )
    weight_copies = []
    for index, (src, dst) in enumerate(zip(sources, far_targets)):
        copy = pltpu.make_async_remote_copy(
            src_ref=src,
            dst_ref=dst,
            send_sem=weight_send.at[index],
            recv_sem=weight_recv.at[index],
            device_id=sibling,
            device_id_type=MESH_ID,
        )
        copy.start()
        weight_copies.append(copy)
    layer_plain = []
    nexts = projected(1)
    layer_out[1] = nexts.astype(bf16)
    for group in range(2):
        layer_plain.append(
            [
                send(
                    layer_out.at[1, pl.ds(group * SUB + HALF, HALF)],
                    layer_side.at[0, group, pl.ds(HALF, HALF)],
                    above,
                )
            ]
        )
    prevs = projected(3)
    layer_out[3] = prevs.astype(bf16)
    for group in range(2):
        layer_plain[group].append(
            send(
                layer_out.at[3, pl.ds(group * SUB, HALF)],
                layer_side.at[1, group, pl.ds(0, HALF)],
                below,
            )
        )
    layer_far = []
    for group in range(2):
        start = group * SUB
        layer_opp[group][0].wait_recv()
        layer_merged[0, group] = (
            layer_out[1, pl.ds(start, HALF)].astype(f32) + layer_opposite[0, group].astype(f32)
        ).astype(bf16)
        a = send(layer_merged.at[0, group], layer_side.at[0, group, pl.ds(0, HALF)], above)
        layer_opp[group][1].wait_recv()
        layer_merged[1, group] = (
            layer_out[3, pl.ds(start + HALF, HALF)].astype(f32)
            + layer_opposite[1, group].astype(f32)
        ).astype(bf16)
        b = send(layer_merged.at[1, group], layer_side.at[1, group, pl.ds(HALF, HALF)], below)
        layer_far.append((a, b))
    residual[...] = projected(0)

    def enter(group):
        for copy in layer_plain[group]:
            copy.wait_recv()
        for copy in layer_far[group]:
            copy.wait_recv()
        rows = pl.ds(group * SUB, SUB)
        total = (
            residual[rows]
            + layer_side[0, group].astype(f32)
            + layer_side[1, group].astype(f32)
        )
        after = own_states[rows].astype(f32) + normed(total, post_gain_ref[...])
        residual[rows] = after
        rows_buf[0, pl.ds(group * RING * SUB, SUB)] = normed(after, ffw_gain_ref[...]).astype(bf16)

    step1 = []
    across = {}

    def send_across(group, sub):
        plus, minus = second[group]
        across[group, sub] = (
            send(slot(group, 0, sub), slot(group, 3, sub), plus),
            send(slot(group, 0, sub), slot(group, 1, sub), minus),
        )

    relays = {}

    def relay_across(group, sub):
        plus, minus = second[group]
        across[group, sub][0].wait_recv()
        a = send(slot(group, 3, sub, 0, HALF), slot(group, 2, sub, 0, HALF), plus)
        across[group, sub][1].wait_recv()
        b = send(slot(group, 1, sub, HALF, HALF), slot(group, 2, sub, HALF, HALF), minus)
        relays[group, sub] = (a, b)

    for group in range(2):
        plus, minus = first[group]
        enter(group)
        step1.append(
            (
                send(slot(group, 0, 0), slot(group, 0, 3), plus),
                send(slot(group, 0, 0), slot(group, 0, 1), minus),
            )
        )
        send_across(group, 0)
    step2 = []
    for group in range(2):
        plus, minus = first[group]
        step1[group][0].wait_recv()
        a = send(slot(group, 0, 3, 0, HALF), slot(group, 0, 2, 0, HALF), plus)
        step1[group][1].wait_recv()
        b = send(slot(group, 0, 1, HALF, HALF), slot(group, 0, 2, HALF, HALF), minus)
        step2.append((a, b))
    for group in range(2):
        send_across(group, 1)
        send_across(group, 3)
    for group in range(2):
        relay_across(group, 0)
    for group in range(2):
        step2[group][0].wait_recv()
        step2[group][1].wait_recv()
        send_across(group, 2)

    for copy in local:
        copy.wait()
    for copy in weight_copies:
        copy.wait_recv()

    def compute(chunk):
        rows = rows_buf[chunk]
        both = lax.dot_general(
            rows, gate_up[...], (((1,), (1,)), ((), ())), preferred_element_type=jnp.float32
        )
        gate = both[:, : 2 * hidden]
        act = (jax.nn.gelu(gate, approximate=True) * both[:, 2 * hidden :]).astype(jnp.bfloat16)
        partial[chunk] = jnp.dot(act, down_w[...], preferred_element_type=jnp.float32).astype(
            jnp.bfloat16
        )

    for group in range(2):
        relay_across(group, 1)
        relay_across(group, 3)
    compute(0)
    for group in range(2):
        relay_across(group, 2)
    compute(1)

    span = RING * SUB
    half = span // 2

    def part(buf, group, chunk, which):
        return buf.at[chunk, pl.ds(group * span + which * half, half)]

    def side(group, which, low):
        return side_in.at[which, pl.ds(group * span + low * half, half)]

    plain = []
    for group in range(2):
        plus, minus = second[group]
        plain.append([send(part(partial, group, 1, 1), side(group, 0, 1), plus)])
    compute(3)
    for group in range(2):
        plus, minus = second[group]
        plain[group].append(send(part(partial, group, 3, 0), side(group, 1, 0), minus))
    for pair in relays.values():
        pair[0].wait_recv()
        pair[1].wait_recv()
    compute(2)
    opposite = []
    for group in range(2):
        plus, minus = second[group]
        opposite.append(
            (
                send(part(partial, group, 2, 0), opposite_in.at[0, pl.ds(group * half, half)], plus),
                send(part(partial, group, 2, 1), opposite_in.at[1, pl.ds(group * half, half)], minus),
            )
        )
    merged = []
    for group in range(2):
        plus, minus = second[group]
        rows = pl.ds(group * half, half)
        opposite[group][0].wait_recv()
        merged_out[0, rows] = (
            part(partial, group, 1, 0)[...].astype(jnp.float32)
            + opposite_in[0, rows].astype(jnp.float32)
        ).astype(jnp.bfloat16)
        a = send(merged_out.at[0, rows], side(group, 0, 0), plus)
        opposite[group][1].wait_recv()
        merged_out[1, rows] = (
            part(partial, group, 3, 1)[...].astype(jnp.float32)
            + opposite_in[1, rows].astype(jnp.float32)
        ).astype(jnp.bfloat16)
        b = send(merged_out.at[1, rows], side(group, 1, 1), minus)
        merged.append((a, b))

    def summed(group, sub):
        rows = pl.ds(group * span + sub * SUB, SUB)
        return (
            partial[0, rows].astype(jnp.float32)
            + side_in[0, rows].astype(jnp.float32)
            + side_in[1, rows].astype(jnp.float32)
        )

    last = []
    for group in range(2):
        plus, minus = first[group]
        plain[group][0].wait_recv()
        merged[group][1].wait_recv()
        send2[group, 2] = summed(group, 2).astype(jnp.bfloat16)
        a = send(send2.at[group, 2, pl.ds(0, HALF)], opposite_in2.at[group, 0], plus)
        b = send(send2.at[group, 2, pl.ds(HALF, HALF)], opposite_in2.at[group, 1], minus)
        last.append([a, b])
    for group in range(2):
        plus, minus = first[group]
        plain[group][1].wait_recv()
        merged[group][0].wait_recv()
        row_sum[group, 0] = summed(group, 1)
        row_sum[group, 1] = summed(group, 3)
        send2[group, 1] = row_sum[group, 0].astype(jnp.bfloat16)
        send2[group, 3] = row_sum[group, 1].astype(jnp.bfloat16)
        a = send(
            send2.at[group, 1, pl.ds(HALF, HALF)], side_in2.at[group, 0, pl.ds(HALF, HALF)], plus
        )
        b = send(send2.at[group, 3, pl.ds(0, HALF)], side_in2.at[group, 1, pl.ds(0, HALF)], minus)
        last[group] += [a, b]
    for group in range(2):
        plus, minus = first[group]
        last[group][0].wait_recv()
        merged_out2[group, 0] = (
            row_sum[group, 0, pl.ds(0, HALF)] + opposite_in2[group, 0].astype(jnp.float32)
        ).astype(jnp.bfloat16)
        a = send(merged_out2.at[group, 0], side_in2.at[group, 0, pl.ds(0, HALF)], plus)
        last[group][1].wait_recv()
        merged_out2[group, 1] = (
            row_sum[group, 1, pl.ds(HALF, HALF)] + opposite_in2[group, 1].astype(jnp.float32)
        ).astype(jnp.bfloat16)
        b = send(merged_out2.at[group, 1], side_in2.at[group, 1, pl.ds(HALF, HALF)], minus)
        last[group] += [a, b]
    for group in range(2):
        own = summed(group, 0)
        for index in (2, 3, 4, 5):
            last[group][index].wait_recv()
        total = own + side_in2[group, 0].astype(jnp.float32) + side_in2[group, 1].astype(jnp.float32)
        rows = pl.ds(group * SUB, SUB)
        out_ref[rows] = (residual[rows] + normed(total, gain_ref[...])).astype(out_ref.dtype)

    for copy in copies:
        copy.wait_send()
    for copy in weight_copies:
        copy.wait_send()


def ffn_block(
    attended, post_gain, ffw_gain, gain, states, out_w, gate_t, up_t, down_weight
):
    width = states.shape[1]
    rows = 2 * SUB
    hidden = gate_t.shape[0]
    vmem = pl.BlockSpec(memory_space=pltpu.VMEM)
    hbm = pl.BlockSpec(memory_space=pl.ANY)
    bf16 = jnp.bfloat16
    span = RING * SUB
    copies = 76
    return pl.pallas_call(
        ffn_kernel,
        out_shape=jax.ShapeDtypeStruct((rows, width), bf16),
        in_specs=[vmem] * 4 + [hbm] * 5,
        out_specs=vmem,
        scratch_shapes=[
            pltpu.VMEM(out_w.shape, bf16),
            pltpu.VMEM((rows, width), bf16),
            pltpu.VMEM((RING, rows, width), bf16),
            pltpu.VMEM((2, 2, HALF, width), bf16),
            pltpu.VMEM((2, 2, HALF, width), bf16),
            pltpu.VMEM((2, 2, SUB, width), bf16),
            pltpu.VMEM((rows, width), jnp.float32),
            pltpu.VMEM((RING, 2 * span, width), bf16),
            pltpu.VMEM((4 * hidden, width), bf16),
            pltpu.VMEM((2 * hidden, width), bf16),
            pltpu.VMEM((RING, 2 * span, width), bf16),
            pltpu.VMEM((2, span, width), bf16),
            pltpu.VMEM((2, span, width), bf16),
            pltpu.VMEM((2, 2 * span, width), bf16),
            pltpu.VMEM((2, 2, SUB, width), jnp.float32),
            pltpu.VMEM((2, 2, HALF, width), bf16),
            pltpu.VMEM((2, RING, SUB, width), bf16),
            pltpu.VMEM((2, 2, HALF, width), bf16),
            pltpu.VMEM((2, 2, SUB, width), bf16),
            pltpu.SemaphoreType.DMA((5,)),
            pltpu.SemaphoreType.DMA((copies,)),
            pltpu.SemaphoreType.DMA((copies,)),
            pltpu.SemaphoreType.DMA((3,)),
            pltpu.SemaphoreType.DMA((3,)),
        ],
        compiler_params=pltpu.CompilerParams(
            collective_id=0, has_side_effects=True, vmem_limit_bytes=58 << 20
        ),
        name="ffn_block",
    )(attended, post_gain, ffw_gain, gain, states, out_w, gate_t, up_t, down_weight)


def plane_place():
    me = lax.axis_index("req")
    layer = lax.axis_index("mlp")
    core = lax.rem(me, 2)
    chip = me // 2
    return chip // RING, lax.rem(chip, RING), core, layer


def attention_kernel(
    states_ref,
    attn_gain_ref,
    query_gain_ref,
    key_gain_ref,
    segment_ref,
    prefix_ref,
    owner_ref,
    query_w_ref,
    key_w_ref,
    value_w_ref,
    keys_ref,
    values_ref,
    out_ref,
    query_w,
    key_w,
    value_w,
    stored_keys,
    stored_values,
    outgoing,
    incoming,
    results,
    back,
    local_sem,
    send_sem,
    recv_sem,
    back_send_sem,
    back_recv_sem,
):
    row, col, core, layer = plane_place()
    rows, width = states_ref.shape
    head = query_gain_ref.shape[1]
    heads = query_w.shape[1] // head
    peers = 2 * RING * RING
    score_scale = head ** (-0.5)
    f32, bf16 = jnp.float32, jnp.bfloat16

    def shifted(offset, sign):
        down, across, flip = offset // (2 * RING), (offset // 2) % RING, offset % 2
        if sign < 0:
            down, across = (RING - down) % RING, (RING - across) % RING
        row_at = lax.rem(row + down, RING)
        col_at = lax.rem(col + across, RING)
        core_at = 1 - core if flip else core
        return ((row_at * RING + col_at) * 2 + core_at, layer)

    barrier = pltpu.get_barrier_semaphore()
    for offset in range(1, peers):
        pl.semaphore_signal(barrier, inc=1, device_id=shifted(offset, 1), device_id_type=MESH_ID)
    local = []
    for index, (src, dst) in enumerate(
        (
            (query_w_ref, query_w),
            (key_w_ref, key_w),
            (value_w_ref, value_w),
            (keys_ref, stored_keys),
            (values_ref, stored_values),
        )
    ):
        copy = pltpu.make_async_copy(src, dst, local_sem.at[index])
        copy.start()
        local.append(copy)

    normalized = normed(states_ref[...].astype(f32), attn_gain_ref[...]).astype(bf16)

    def column(line):
        return jnp.transpose(jnp.broadcast_to(line, (128, rows)))[:, :1]

    prefix_row = prefix_ref[...].astype(f32)
    prefix_col = column(prefix_row)
    row_at = lax.broadcasted_iota(jnp.int32, (rows, rows), 0)
    col_at = lax.broadcasted_iota(jnp.int32, (rows, rows), 1)
    same = jnp.where(prefix_col == prefix_row, 1.0, 0.0)
    rank_col = jnp.sum(jnp.where(col_at < row_at, same, 0.0), axis=1, keepdims=True)
    rank_row = jnp.sum(jnp.where(row_at < col_at, same, 0.0), axis=0, keepdims=True)
    groups = owner_ref.shape[1]
    onehot = prefix_col == lax.broadcasted_iota(jnp.int32, (rows, groups), 1).astype(f32)
    owner_col = jnp.sum(jnp.where(onehot, owner_ref[...].astype(f32), 0.0), axis=1, keepdims=True)
    owner_row = jnp.transpose(jnp.broadcast_to(owner_col, (rows, 128)))[:1]

    def place(owner, rank):
        owner = owner.astype(jnp.int32)
        down = ((owner >> 3) - row) & 3
        across = (((owner >> 1) & 3) - col) & 3
        flip = ((owner & 1) - core) & 1
        return (down * 8 + across * 2 + flip) * CAP + rank.astype(jnp.int32)

    place_col = place(owner_col, rank_col)
    place_row = place(owner_row, rank_row)

    local[0].wait()
    raw = jnp.dot(normalized, query_w[...], preferred_element_type=f32)
    queries = [
        normed(raw[:, g * head : (g + 1) * head], query_gain_ref[...]).astype(bf16)
        for g in range(heads)
    ]
    query_rows = jnp.concatenate(queries, axis=1)
    pl.semaphore_wait(barrier, peers - 1)
    sends = {}
    batch = 2 * RING
    for part in range(peers // batch):
        slots = lax.broadcasted_iota(jnp.int32, (batch * CAP, rows), 0) + part * batch * CAP
        placing = jnp.where(slots == place_row, 1.0, 0.0).astype(bf16)
        packed = jnp.dot(placing, query_rows, preferred_element_type=f32).astype(bf16)
        packed = packed.reshape(batch, CAP, heads * head)
        if part == 0:
            incoming[0] = packed[0]
        outgoing[pl.ds(part * batch, batch)] = packed
        for offset in range(max(part * batch, 1), (part + 1) * batch):
            copy = pltpu.make_async_remote_copy(
                src_ref=outgoing.at[offset],
                dst_ref=incoming.at[offset],
                send_sem=send_sem.at[offset],
                recv_sem=recv_sem.at[offset],
                device_id=shifted(offset, 1),
                device_id_type=MESH_ID,
            )
            copy.start()
            sends[offset] = copy

    local[1].wait()
    local[2].wait()
    raw = jnp.dot(normalized, key_w[...], preferred_element_type=f32)
    keys = normed(raw, key_gain_ref[...]).astype(bf16)
    values = jnp.dot(normalized, value_w[...], preferred_element_type=f32).astype(bf16)
    segment_row = segment_ref[...].astype(f32)
    allowed = (column(segment_row) == segment_row) & (row_at >= col_at)

    def attend(query, key, value, mask):
        scores = (
            lax.dot_general(query, key, (((1,), (1,)), ((), ())), preferred_element_type=f32)
            * score_scale
        )
        if mask is not None:
            scores = jnp.where(mask, scores, -jnp.inf)
        row_max = jnp.max(scores, axis=-1, keepdims=True)
        powers = jnp.exp(scores - row_max)
        total = jnp.sum(powers, axis=-1, keepdims=True)
        weights = (powers / total).astype(bf16)
        mixed = jnp.dot(weights, value, preferred_element_type=f32)
        return mixed, row_max + jnp.log(total)

    suffix = [attend(query, keys, values, allowed) for query in queries]

    local[3].wait()
    local[4].wait()
    lanes = lax.broadcasted_iota(jnp.int32, (batch * CAP, 128), 1)
    returns = {}
    for part in range(peers // batch):
        for offset in range(max(part * batch, 1), (part + 1) * batch):
            sends[offset].wait_recv()
        query = incoming[pl.ds(part * batch, batch)].reshape(batch * CAP, heads * head)
        tail = jnp.zeros((batch * CAP, 128), f32)
        for g in range(heads):
            mixed, log_total = attend(
                query[:, g * head : (g + 1) * head], stored_keys[...], stored_values[...], None
            )
            coarse = log_total.astype(bf16).astype(f32)
            tail = jnp.where(lanes == 2 * g, coarse, tail)
            tail = jnp.where(lanes == 2 * g + 1, log_total - coarse, tail)
            results[pl.ds(part * batch, batch), :, pl.ds(g * head, head)] = mixed.astype(
                bf16
            ).reshape(batch, CAP, head)
        results[pl.ds(part * batch, batch), :, pl.ds(heads * head, 128)] = tail.astype(
            bf16
        ).reshape(batch, CAP, 128)
        if part == 0:
            back[0] = results[0]
        for offset in range(max(part * batch, 1), (part + 1) * batch):
            copy = pltpu.make_async_remote_copy(
                src_ref=results.at[offset],
                dst_ref=back.at[offset],
                send_sem=back_send_sem.at[offset],
                recv_sem=back_recv_sem.at[offset],
                device_id=shifted(offset, -1),
                device_id_type=MESH_ID,
            )
            copy.start()
            returns[offset] = copy

    picked = jnp.zeros((rows, heads * head + 128), f32)
    for part in range(peers // batch):
        for offset in range(max(part * batch, 1), (part + 1) * batch):
            returns[offset].wait_recv()
        slots = lax.broadcasted_iota(jnp.int32, (rows, batch * CAP), 1) + part * batch * CAP
        choosing = jnp.where(slots == place_col, 1.0, 0.0).astype(bf16)
        block = back[pl.ds(part * batch, batch)].reshape(batch * CAP, heads * head + 128)
        picked = picked + jnp.dot(choosing, block, preferred_element_type=f32)
    for g in range(heads):
        mixed, log_total = suffix[g]
        at = heads * head + 2 * g
        prefix_lse = picked[:, at : at + 1] + picked[:, at + 1 : at + 2]
        blend = jax.nn.sigmoid(prefix_lse - log_total)
        columns = slice(g * head, (g + 1) * head)
        out_ref[:, columns] = (blend * picked[:, columns] + (1.0 - blend) * mixed).astype(bf16)

    for offset in range(1, peers):
        sends[offset].wait_send()
        returns[offset].wait_send()


def attention_block(
    states, attn_gain, query_gain, key_gain, segment, prefix_id, owner_map, query_w, key_w, value_w, keys, values
):
    rows, width = states.shape
    vmem = pl.BlockSpec(memory_space=pltpu.VMEM)
    hbm = pl.BlockSpec(memory_space=pl.ANY)
    bf16 = jnp.bfloat16
    peers = 2 * RING * RING
    cols = query_w.shape[1]
    return pl.pallas_call(
        attention_kernel,
        out_shape=jax.ShapeDtypeStruct((rows, cols), bf16),
        in_specs=[vmem] * 7 + [hbm] * 5,
        out_specs=vmem,
        scratch_shapes=[
            pltpu.VMEM(query_w.shape, bf16),
            pltpu.VMEM(key_w.shape, bf16),
            pltpu.VMEM(value_w.shape, bf16),
            pltpu.VMEM(keys.shape, bf16),
            pltpu.VMEM(values.shape, bf16),
            pltpu.VMEM((peers, CAP, cols), bf16),
            pltpu.VMEM((peers, CAP, cols), bf16),
            pltpu.VMEM((peers, CAP, cols + 128), bf16),
            pltpu.VMEM((peers, CAP, cols + 128), bf16),
            pltpu.SemaphoreType.DMA((5,)),
            pltpu.SemaphoreType.DMA((peers,)),
            pltpu.SemaphoreType.DMA((peers,)),
            pltpu.SemaphoreType.DMA((peers,)),
            pltpu.SemaphoreType.DMA((peers,)),
        ],
        compiler_params=pltpu.CompilerParams(
            collective_id=1, has_side_effects=True, vmem_limit_bytes=58 << 20
        ),
        name="attention_block",
    )(
        states,
        attn_gain,
        query_gain,
        key_gain,
        segment,
        prefix_id,
        owner_map,
        query_w,
        key_w,
        value_w,
        keys,
        values,
    )


def body(
    states,
    attn_gain,
    query_matrix,
    key_matrix,
    value_matrix,
    query_gain,
    key_gain,
    out_weight,
    post_gain,
    ffw_gain,
    gate_weight,
    up_weight,
    down_weight,
    post_ffw_gain,
    prefix_key_cache,
    prefix_value_cache,
    segment,
    prefix_id,
    owner_map,
):
    attended = attention_block(
        states,
        attn_gain[None],
        query_gain[None],
        key_gain[None],
        segment[None],
        prefix_id[None],
        owner_map[None],
        query_matrix,
        key_matrix,
        value_matrix,
        prefix_key_cache[0],
        prefix_value_cache[0],
    )
    return ffn_block(
        attended,
        post_gain[None],
        ffw_gain[None],
        post_ffw_gain[None],
        states,
        out_weight,
        gate_weight.T,
        up_weight.T,
        down_weight,
    )


def solution(mesh):
    return jax.shard_map(
        body,
        mesh=mesh,
        in_specs=(
            P("req", None),
            P(),
            P(None, "mlp"),
            P(None, "mlp"),
            P(None, "mlp"),
            P(),
            P(),
            P("mlp", None),
            P(),
            P(),
            P(None, "req"),
            P(None, "req"),
            P("req", None),
            P(),
            P("req", None, "mlp"),
            P("req", None, "mlp"),
            P("req"),
            P("req"),
            P(),
        ),
        out_specs=P(("req", "mlp"), None),
        check_vma=False,
    )
```

```python
import jax
import jax.numpy as jnp
from jax import lax
from jax.experimental import pallas as pl
from jax.experimental.pallas import tpu as pltpu
from jax.sharding import PartitionSpec as P

EPS = 1e-06

MESH_ID = pl.DeviceIdType.MESH
RING = 4
SUB = 32
HALF = 16
CAP = 16
PEERS = 2 * RING * RING
PART = 16
SPAN = RING * SUB
ORDER = (2, 1, 3, 0)


def normed(values_in, gain_vec):
    return (
        values_in
        * lax.rsqrt(jnp.mean(values_in * values_in, axis=-1, keepdims=True) + EPS)
        * gain_vec
    )


def layer_kernel(
    states_ref,
    attn_gain_ref,
    query_gain_ref,
    key_gain_ref,
    segment_ref,
    prefix_ref,
    owner_ref,
    post_gain_ref,
    ffw_gain_ref,
    last_gain_ref,
    query_w_ref,
    key_w_ref,
    value_w_ref,
    keys_ref,
    values_ref,
    out_w_ref,
    gate_ref,
    up_ref,
    down_ref,
    out_ref,
    query_w,
    key_w,
    value_w,
    stored_keys,
    stored_values,
    outgoing,
    incoming,
    results,
    back,
    out_w,
    projected,
    layer_out,
    layer_opposite,
    layer_merged,
    layer_side,
    residual,
    rows_buf,
    gate_up,
    down_w,
    partial,
    opposite_in,
    merged_out,
    side_in,
    row_sum,
    send2,
    opposite_in2,
    merged_out2,
    side_in2,
    local_sem,
    query_send_sem,
    query_recv_sem,
    back_send_sem,
    back_recv_sem,
    weight_send,
    weight_recv,
    send_sem,
    recv_sem,
):
    me = lax.axis_index("req")
    layer = lax.axis_index("mlp")
    core = lax.rem(me, 2)
    chip = me // 2
    row, col = chip // RING, lax.rem(chip, RING)
    rows, width = states_ref.shape
    head = query_gain_ref.shape[1]
    heads = query_w.shape[1] // head
    cols = heads * head
    hidden = gate_ref.shape[0]
    quarter = 2 * SUB
    score_scale = head ** (-0.5)
    f32, bf16 = jnp.float32, jnp.bfloat16

    def shifted(offset, sign=1):
        down, across, flip = offset // (2 * RING), (offset // 2) % RING, offset % 2
        if sign < 0:
            down, across = (RING - down) % RING, (RING - across) % RING
        row_at = lax.rem(row + down, RING)
        col_at = lax.rem(col + across, RING)
        core_at = 1 - core if flip else core
        return ((row_at * RING + col_at) * 2 + core_at, layer)

    right, left, sibling = shifted(2), shifted(2, -1), shifted(1)
    upper, lower = shifted(2 * RING), shifted(2 * RING, -1)
    above = (me, lax.rem(layer + 1, RING))
    below = (me, lax.rem(layer + RING - 1, RING))

    barrier = pltpu.get_barrier_semaphore()
    for offset in range(1, PEERS):
        pl.semaphore_signal(barrier, inc=1, device_id=shifted(offset), device_id_type=MESH_ID)
    for peer in (above, below):
        pl.semaphore_signal(barrier, inc=1, device_id=peer, device_id_type=MESH_ID)

    sources = (gate_ref, up_ref, down_ref)
    targets = (
        gate_up.at[pl.ds(0, hidden)],
        gate_up.at[pl.ds(2 * hidden, hidden)],
        down_w.at[pl.ds(0, hidden)],
    )
    far_targets = (
        gate_up.at[pl.ds(hidden, hidden)],
        gate_up.at[pl.ds(3 * hidden, hidden)],
        down_w.at[pl.ds(hidden, hidden)],
    )
    local = []
    for index, (src, dst) in enumerate(
        (
            (query_w_ref, query_w),
            (key_w_ref, key_w),
            (value_w_ref, value_w),
            (keys_ref, stored_keys),
            (values_ref, stored_values),
            (out_w_ref, out_w),
        )
        + tuple(zip(sources, targets))
    ):
        copy = pltpu.make_async_copy(src, dst, local_sem.at[index])
        copy.start()
        local.append(copy)

    def line(ref):
        return jnp.concatenate([ref[i : i + 1] for i in range(ref.shape[0])], axis=1)

    normalized = normed(states_ref[...].astype(f32), line(attn_gain_ref)).astype(bf16)

    def column(values):
        return jnp.transpose(jnp.broadcast_to(values, (128, rows)))[:, :1]

    prefix_row = prefix_ref[...].astype(f32)
    prefix_col = column(prefix_row)
    row_at = lax.broadcasted_iota(jnp.int32, (rows, rows), 0)
    col_at = lax.broadcasted_iota(jnp.int32, (rows, rows), 1)
    same = jnp.where(
        (prefix_col == prefix_row) & (((row_at >> 3) & 1) == ((col_at >> 3) & 1)), 1.0, 0.0
    )
    rank_col = jnp.sum(jnp.where(col_at < row_at, same, 0.0), axis=1, keepdims=True)
    rank_row = jnp.sum(jnp.where(row_at < col_at, same, 0.0), axis=0, keepdims=True)
    groups = owner_ref.shape[1]
    onehot = prefix_col == lax.broadcasted_iota(jnp.int32, (rows, groups), 1).astype(f32)
    owner_col = jnp.sum(jnp.where(onehot, owner_ref[...].astype(f32), 0.0), axis=1, keepdims=True)
    owner_row = jnp.transpose(jnp.broadcast_to(owner_col, (rows, 128)))[:1]

    def place(owner, rank):
        owner = owner.astype(jnp.int32)
        down = ((owner >> 3) - row) & 3
        across = (((owner >> 1) & 3) - col) & 3
        flip = ((owner & 1) - core) & 1
        return (down * 8 + across * 2 + flip) * CAP + rank.astype(jnp.int32)

    place_col = place(owner_col, rank_col)
    place_row = place(owner_row, rank_row)
    set_row = (lax.broadcasted_iota(jnp.int32, (1, rows), 1) >> 3) & 1

    def of_set(values, group):
        count, lanes = values.shape
        return values.reshape(count // 16, 2, 8, lanes)[:, group].reshape(count // 2, lanes)

    local[0].wait()
    raw = jnp.dot(normalized, query_w[...], preferred_element_type=f32)
    queries = [
        normed(raw[:, g * head : (g + 1) * head], query_gain_ref[...]).astype(bf16)
        for g in range(heads)
    ]
    query_rows = jnp.concatenate(queries, axis=1)
    pl.semaphore_wait(barrier, PEERS + 1)
    slot_at = lax.broadcasted_iota(jnp.int32, (PART * CAP, rows), 0)
    for group in range(2):
        goal = jnp.where(set_row == group, place_row, -1)
        for part in range(PEERS // PART):
            placing = jnp.where(slot_at + part * PART * CAP == goal, 1.0, 0.0).astype(bf16)
            packed = jnp.dot(placing, query_rows, preferred_element_type=f32).astype(bf16)
            packed = packed.reshape(PART, CAP, cols)
            if part == 0:
                incoming[group, 0] = packed[0]
            outgoing[group, pl.ds(part * PART, PART)] = packed
            for offset in range(max(part * PART, 1), (part + 1) * PART):
                pltpu.make_async_remote_copy(
                    src_ref=outgoing.at[group, offset],
                    dst_ref=incoming.at[group, offset],
                    send_sem=query_send_sem.at[group],
                    recv_sem=query_recv_sem.at[group, part],
                    device_id=shifted(offset),
                    device_id_type=MESH_ID,
                ).start()
    weight_copies = []
    for index, (src, dst) in enumerate(zip(sources, far_targets)):
        copy = pltpu.make_async_remote_copy(
            src_ref=src,
            dst_ref=dst,
            send_sem=weight_send.at[index],
            recv_sem=weight_recv.at[index],
            device_id=sibling,
            device_id_type=MESH_ID,
        )
        copy.start()
        weight_copies.append(copy)

    local[1].wait()
    local[2].wait()
    raw = jnp.dot(normalized, key_w[...], preferred_element_type=f32)
    keys = normed(raw, key_gain_ref[...]).astype(bf16)
    values = jnp.dot(normalized, value_w[...], preferred_element_type=f32).astype(bf16)
    segment_row = segment_ref[...].astype(f32)
    allowed = (column(segment_row) == segment_row) & (row_at >= col_at)

    def attend(query, key, value, mask):
        scores = (
            lax.dot_general(query, key, (((1,), (1,)), ((), ())), preferred_element_type=f32)
            * score_scale
        )
        if mask is not None:
            scores = jnp.where(mask, scores, -jnp.inf)
        row_max = jnp.max(scores, axis=-1, keepdims=True)
        powers = jnp.exp(scores - row_max)
        total = jnp.sum(powers, axis=-1, keepdims=True)
        weights = (powers / total).astype(bf16)
        mixed = jnp.dot(weights, value, preferred_element_type=f32)
        return mixed, row_max + jnp.log(total)

    suffix = [attend(query, keys, values, allowed) for query in queries]

    def remote_blocks(buf, group, part):
        start = max(part * PART, 1)
        return buf.at[group, pl.ds(start, (part + 1) * PART - start)]

    def await_blocks(buf, group, part, sem):
        blocks = remote_blocks(buf, group, part)
        pltpu.make_async_copy(blocks, blocks, sem).wait()

    local[3].wait()
    local[4].wait()
    lanes = lax.broadcasted_iota(jnp.int32, (PART * CAP, 128), 1)
    for group in range(2):
        for part in range(PEERS // PART):
            await_blocks(incoming, group, part, query_recv_sem.at[group, part])
            blocks = pl.ds(part * PART, PART)
            query = incoming[group, blocks].reshape(PART * CAP, cols)
            tail = jnp.zeros((PART * CAP, 128), f32)
            for g in range(heads):
                mixed, log_total = attend(
                    query[:, g * head : (g + 1) * head], stored_keys[...], stored_values[...], None
                )
                coarse = log_total.astype(bf16).astype(f32)
                tail = jnp.where(lanes == 2 * g, coarse, tail)
                tail = jnp.where(lanes == 2 * g + 1, log_total - coarse, tail)
                results[group, blocks, :, pl.ds(g * head, head)] = mixed.astype(bf16).reshape(
                    PART, CAP, head
                )
            results[group, blocks, :, pl.ds(cols, 128)] = tail.astype(bf16).reshape(
                PART, CAP, 128
            )
            if part == 0:
                back[group, 0] = results[group, 0]
            for offset in range(max(part * PART, 1), (part + 1) * PART):
                pltpu.make_async_remote_copy(
                    src_ref=results.at[group, offset],
                    dst_ref=back.at[group, offset],
                    send_sem=back_send_sem.at[group],
                    recv_sem=back_recv_sem.at[group, part],
                    device_id=shifted(offset, -1),
                    device_id_type=MESH_ID,
                ).start()

    copies = []

    def send(src, dst, peer):
        index = len(copies)
        copy = pltpu.make_async_remote_copy(
            src_ref=src,
            dst_ref=dst,
            send_sem=send_sem.at[index],
            recv_sem=recv_sem.at[index],
            device_id=peer,
            device_id_type=MESH_ID,
        )
        copy.start()
        copies.append(copy)
        return copy

    def quarter_rows(ref, group, offset, start, size):
        at = lax.rem(layer + offset, RING) * SUB + start
        return ref.at[group, pl.ds(pl.multiple_of(at, HALF), size)]

    layer_opp, layer_plain, layer_far = {}, {}, {}

    def project(group):
        picked = jnp.zeros((rows // 2, cols + 128), f32)
        places = of_set(place_col, group)
        for part in range(PEERS // PART):
            await_blocks(back, group, part, back_recv_sem.at[group, part])
            slots = lax.broadcasted_iota(jnp.int32, (rows // 2, PART * CAP), 1)
            choosing = jnp.where(slots + part * PART * CAP == places, 1.0, 0.0).astype(bf16)
            block = back[group, pl.ds(part * PART, PART)].reshape(PART * CAP, cols + 128)
            picked = picked + jnp.dot(choosing, block, preferred_element_type=f32)
        attended = []
        for g in range(heads):
            mixed, log_total = suffix[g]
            at = cols + 2 * g
            prefix_lse = picked[:, at : at + 1] + picked[:, at + 1 : at + 2]
            blend = jax.nn.sigmoid(prefix_lse - of_set(log_total, group))
            attended.append(
                (
                    blend * picked[:, g * head : (g + 1) * head]
                    + (1.0 - blend) * of_set(mixed, group)
                ).astype(bf16)
            )
        out = jnp.dot(jnp.concatenate(attended, axis=1), out_w[...], preferred_element_type=f32)
        projected[group] = out
        layer_out[group] = out.astype(bf16)
        layer_opp[group] = (
            send(quarter_rows(layer_out, group, 2, 0, HALF), layer_opposite.at[0, group], above),
            send(quarter_rows(layer_out, group, 2, HALF, HALF), layer_opposite.at[1, group], below),
        )
        layer_plain[group] = (
            send(
                quarter_rows(layer_out, group, 1, HALF, HALF),
                layer_side.at[0, group, pl.ds(HALF, HALF)],
                above,
            ),
            send(
                quarter_rows(layer_out, group, 3, 0, HALF),
                layer_side.at[1, group, pl.ds(0, HALF)],
                below,
            ),
        )

    def merge_layers(group):
        layer_opp[group][0].wait_recv()
        layer_merged[0, group] = (
            quarter_rows(projected, group, 1, 0, HALF)[...] + layer_opposite[0, group].astype(f32)
        ).astype(bf16)
        a = send(layer_merged.at[0, group], layer_side.at[0, group, pl.ds(0, HALF)], above)
        layer_opp[group][1].wait_recv()
        layer_merged[1, group] = (
            quarter_rows(projected, group, 3, HALF, HALF)[...]
            + layer_opposite[1, group].astype(f32)
        ).astype(bf16)
        b = send(layer_merged.at[1, group], layer_side.at[1, group, pl.ds(HALF, HALF)], below)
        layer_far[group] = (a, b)

    first = ((right, left), (upper, lower))
    second = ((upper, lower), (right, left))
    step1, step2, across, relays = {}, {}, {}, {}

    def slot(group, chunk, sub, start=0, size=SUB):
        return rows_buf.at[chunk, pl.ds(group * SPAN + sub * SUB + start, size)]

    def send_across(group, sub):
        plus, minus = second[group]
        across[group, sub] = (
            send(slot(group, 0, sub), slot(group, 3, sub), plus),
            send(slot(group, 0, sub), slot(group, 1, sub), minus),
        )

    def relay_across(group, sub):
        plus, minus = second[group]
        across[group, sub][0].wait_recv()
        a = send(slot(group, 3, sub, 0, HALF), slot(group, 2, sub, 0, HALF), plus)
        across[group, sub][1].wait_recv()
        b = send(slot(group, 1, sub, HALF, HALF), slot(group, 2, sub, HALF, HALF), minus)
        relays[group, sub] = (a, b)

    def enter(group):
        for copy in layer_plain[group] + layer_far[group]:
            copy.wait_recv()
        total = (
            quarter_rows(projected, group, 0, 0, SUB)[...]
            + layer_side[0, group].astype(f32)
            + layer_side[1, group].astype(f32)
        )
        own = states_ref[pl.ds(pl.multiple_of(layer * quarter, quarter), quarter)].astype(f32)
        after = of_set(own, group) + normed(total, line(post_gain_ref))
        residual[group] = after
        rows_buf[0, pl.ds(group * SPAN, SUB)] = normed(after, line(ffw_gain_ref)).astype(bf16)
        plus, minus = first[group]
        step1[group] = (
            send(slot(group, 0, 0), slot(group, 0, 3), plus),
            send(slot(group, 0, 0), slot(group, 0, 1), minus),
        )
        send_across(group, 0)

    def spread(group):
        plus, minus = first[group]
        step1[group][0].wait_recv()
        a = send(slot(group, 0, 3, 0, HALF), slot(group, 0, 2, 0, HALF), plus)
        step1[group][1].wait_recv()
        b = send(slot(group, 0, 1, HALF, HALF), slot(group, 0, 2, HALF, HALF), minus)
        step2[group] = (a, b)
        send_across(group, 1)
        send_across(group, 3)

    def finish_spread(group):
        for copy in step2[group]:
            copy.wait_recv()
        send_across(group, 2)

    def compute(chunk, start, size):
        span = pl.ds(start, size)
        both = lax.dot_general(
            rows_buf[chunk, span],
            gate_up[...],
            (((1,), (1,)), ((), ())),
            preferred_element_type=f32,
        )
        gate = both[:, : 2 * hidden]
        act = (jax.nn.gelu(gate, approximate=True) * both[:, 2 * hidden :]).astype(bf16)
        partial[chunk, span] = jnp.dot(act, down_w[...], preferred_element_type=f32).astype(bf16)

    local[5].wait()
    project(0)
    merge_layers(0)
    project(1)
    enter(0)
    merge_layers(1)
    spread(0)
    relay_across(0, 0)
    enter(1)
    finish_spread(0)
    spread(1)
    relay_across(0, 1)
    relay_across(0, 3)
    relay_across(1, 0)
    finish_spread(1)
    for copy in local[6:]:
        copy.wait()
    for copy in weight_copies:
        copy.wait_recv()
    relay_across(0, 2)
    relay_across(1, 1)
    relay_across(1, 3)
    compute(0, 0, 2 * SPAN)
    relay_across(1, 2)
    compute(1, 0, 2 * SPAN)
    compute(3, 0, 2 * SPAN)

    opposite, plain, merged, last = {}, {}, {}, {}

    def piece(group, chunk, sub, start):
        return partial.at[chunk, pl.ds(group * SPAN + sub * SUB + start, HALF)]

    def side(group, which, sub, start):
        return side_in.at[which, group, sub, pl.ds(start, HALF)]

    def send_opposite(group):
        plus, minus = second[group]
        for sub in ORDER:
            opposite[group, sub] = (
                send(piece(group, 2, sub, 0), opposite_in.at[0, group, sub], plus),
                send(piece(group, 2, sub, HALF), opposite_in.at[1, group, sub], minus),
            )

    def send_plain(group):
        plus, minus = second[group]
        for sub in ORDER:
            plain[group, sub] = (
                send(piece(group, 1, sub, HALF), side(group, 0, sub, HALF), plus),
                send(piece(group, 3, sub, 0), side(group, 1, sub, 0), minus),
            )

    def merge(group, sub):
        plus, minus = second[group]
        opposite[group, sub][0].wait_recv()
        merged_out[0, group, sub] = (
            piece(group, 1, sub, 0)[...].astype(f32) + opposite_in[0, group, sub].astype(f32)
        ).astype(bf16)
        a = send(merged_out.at[0, group, sub], side(group, 0, sub, 0), plus)
        opposite[group, sub][1].wait_recv()
        merged_out[1, group, sub] = (
            piece(group, 3, sub, HALF)[...].astype(f32) + opposite_in[1, group, sub].astype(f32)
        ).astype(bf16)
        b = send(merged_out.at[1, group, sub], side(group, 1, sub, HALF), minus)
        merged[group, sub] = (a, b)

    def summed(group, sub):
        for copy in plain[group, sub] + merged[group, sub]:
            copy.wait_recv()
        return (
            partial[0, pl.ds(group * SPAN + sub * SUB, SUB)].astype(f32)
            + side_in[0, group, sub].astype(f32)
            + side_in[1, group, sub].astype(f32)
        )

    def turn_opposite(group):
        plus, minus = first[group]
        send2[group, 2] = summed(group, 2).astype(bf16)
        last[group, 0] = send(
            send2.at[group, 2, pl.ds(0, HALF)], opposite_in2.at[group, 0], plus
        )
        last[group, 1] = send(
            send2.at[group, 2, pl.ds(HALF, HALF)], opposite_in2.at[group, 1], minus
        )

    def turn_side(group, which):
        sub = (1, 3)[which]
        start = (HALF, 0)[which]
        row_sum[group, which] = summed(group, sub)
        send2[group, sub] = row_sum[group, which].astype(bf16)
        last[group, 2 + which] = send(
            send2.at[group, sub, pl.ds(start, HALF)],
            side_in2.at[group, which, pl.ds(start, HALF)],
            first[group][which],
        )

    def turn_merge(group, which):
        start = (0, HALF)[which]
        last[group, which].wait_recv()
        merged_out2[group, which] = (
            row_sum[group, which, pl.ds(start, HALF)] + opposite_in2[group, which].astype(f32)
        ).astype(bf16)
        last[group, 4 + which] = send(
            merged_out2.at[group, which],
            side_in2.at[group, which, pl.ds(start, HALF)],
            first[group][which],
        )

    def finish(group):
        own = summed(group, 0)
        for index in (2, 3, 4, 5):
            last[group, index].wait_recv()
        total = own + side_in2[group, 0].astype(f32) + side_in2[group, 1].astype(f32)
        return residual[group] + normed(total, line(last_gain_ref))

    send_plain(0)
    for sub in range(RING):
        relays[0, sub][0].wait_recv()
        relays[0, sub][1].wait_recv()
    compute(2, 0, SPAN)
    send_opposite(0)
    send_plain(1)
    for sub in range(RING):
        relays[1, sub][0].wait_recv()
        relays[1, sub][1].wait_recv()
    compute(2, SPAN, SPAN)
    send_opposite(1)
    for sub in ORDER:
        merge(0, sub)
    for sub in ORDER:
        merge(1, sub)
    for group in range(2):
        turn_opposite(group)
        turn_side(group, 0)
        turn_side(group, 1)
        turn_merge(group, 0)
        turn_merge(group, 1)
    ends = [finish(group).reshape(RING, 1, 8, width) for group in range(2)]
    out_ref[...] = jnp.concatenate(ends, axis=1).reshape(quarter, width).astype(out_ref.dtype)

    for group in range(2):
        for buf, sem in ((outgoing, query_send_sem), (results, back_send_sem)):
            blocks = buf.at[group, pl.ds(1, PEERS - 1)]
            pltpu.make_async_copy(blocks, blocks, sem.at[group]).wait()
    for copy in copies + weight_copies:
        copy.wait_send()


def body(
    states,
    attn_gain,
    query_matrix,
    key_matrix,
    value_matrix,
    query_gain,
    key_gain,
    out_weight,
    post_gain,
    ffw_gain,
    gate_weight,
    up_weight,
    down_weight,
    post_ffw_gain,
    prefix_key_cache,
    prefix_value_cache,
    segment,
    prefix_id,
    owner_map,
):
    rows, width = states.shape
    cols = query_matrix.shape[1]
    hidden = gate_weight.shape[1]
    keys, values = prefix_key_cache[0], prefix_value_cache[0]
    vmem = pl.BlockSpec(memory_space=pltpu.VMEM)
    hbm = pl.BlockSpec(memory_space=pl.ANY)
    f32, bf16 = jnp.float32, jnp.bfloat16
    links = 112
    dma = pltpu.SemaphoreType.DMA
    return pl.pallas_call(
        layer_kernel,
        out_shape=jax.ShapeDtypeStruct((2 * SUB, width), bf16),
        in_specs=[vmem] * 10 + [hbm] * 9,
        out_specs=vmem,
        scratch_shapes=[
            pltpu.VMEM(query_matrix.shape, bf16),
            pltpu.VMEM(key_matrix.shape, bf16),
            pltpu.VMEM(value_matrix.shape, bf16),
            pltpu.VMEM(keys.shape, bf16),
            pltpu.VMEM(values.shape, bf16),
            pltpu.VMEM((2, PEERS, CAP, cols), bf16),
            pltpu.VMEM((2, PEERS, CAP, cols), bf16),
            pltpu.VMEM((2, PEERS, CAP, cols + 128), bf16),
            pltpu.VMEM((2, PEERS, CAP, cols + 128), bf16),
            pltpu.VMEM(out_weight.shape, bf16),
            pltpu.VMEM((2, SPAN, width), f32),
            pltpu.VMEM((2, SPAN, width), bf16),
            pltpu.VMEM((2, 2, HALF, width), bf16),
            pltpu.VMEM((2, 2, HALF, width), bf16),
            pltpu.VMEM((2, 2, SUB, width), bf16),
            pltpu.VMEM((2, SUB, width), f32),
            pltpu.VMEM((RING, 2 * SPAN, width), bf16),
            pltpu.VMEM((4 * hidden, width), bf16),
            pltpu.VMEM((2 * hidden, width), bf16),
            pltpu.VMEM((RING, 2 * SPAN, width), bf16),
            pltpu.VMEM((2, 2, RING, HALF, width), bf16),
            pltpu.VMEM((2, 2, RING, HALF, width), bf16),
            pltpu.VMEM((2, 2, RING, SUB, width), bf16),
            pltpu.VMEM((2, 2, SUB, width), f32),
            pltpu.VMEM((2, RING, SUB, width), bf16),
            pltpu.VMEM((2, 2, HALF, width), bf16),
            pltpu.VMEM((2, 2, HALF, width), bf16),
            pltpu.VMEM((2, 2, SUB, width), bf16),
            dma((9,)),
            dma((2,)),
            dma((2, 2)),
            dma((2,)),
            dma((2, 2)),
            dma((3,)),
            dma((3,)),
            dma((links,)),
            dma((links,)),
        ],
        compiler_params=pltpu.CompilerParams(
            collective_id=0, has_side_effects=True, vmem_limit_bytes=60 << 20
        ),
        name="layer",
    )(
        states,
        attn_gain.reshape(-1, 128),
        query_gain[None],
        key_gain[None],
        segment[None],
        prefix_id[None],
        owner_map[None],
        post_gain.reshape(-1, 128),
        ffw_gain.reshape(-1, 128),
        post_ffw_gain.reshape(-1, 128),
        query_matrix,
        key_matrix,
        value_matrix,
        keys,
        values,
        out_weight,
        gate_weight.T,
        up_weight.T,
        down_weight,
    )


def solution(mesh):
    return jax.shard_map(
        body,
        mesh=mesh,
        in_specs=(
            P("req", None),
            P(),
            P(None, "mlp"),
            P(None, "mlp"),
            P(None, "mlp"),
            P(),
            P(),
            P("mlp", None),
            P(),
            P(),
            P(None, "req"),
            P(None, "req"),
            P("req", None),
            P(),
            P("req", None, "mlp"),
            P("req", None, "mlp"),
            P("req"),
            P("req"),
            P(),
        ),
        out_specs=P(("req", "mlp"), None),
        check_vma=False,
    )
```

```python
import jax
import jax.numpy as jnp
from jax import lax
from jax.experimental import pallas as pl
from jax.experimental.pallas import tpu as pltpu
from jax.sharding import PartitionSpec as P

EPS = 1e-06

MESH_ID = pl.DeviceIdType.MESH
RING = 4
SUB = 32
HALF = 16
CAP = 16
PEERS = 2 * RING * RING
PART = 16
SPAN = RING * SUB
ORDER = (2, 1, 3, 0)


def normed(values_in, gain_vec):
    return (
        values_in
        * lax.rsqrt(jnp.mean(values_in * values_in, axis=-1, keepdims=True) + EPS)
        * gain_vec
    )


def layer_kernel(
    states_ref,
    attn_gain_ref,
    query_gain_ref,
    key_gain_ref,
    segment_ref,
    prefix_ref,
    owner_ref,
    post_gain_ref,
    ffw_gain_ref,
    last_gain_ref,
    query_w_ref,
    key_w_ref,
    value_w_ref,
    keys_ref,
    values_ref,
    out_w_ref,
    gate_ref,
    up_ref,
    down_ref,
    out_ref,
    query_w,
    key_w,
    value_w,
    stored_keys,
    stored_values,
    outgoing,
    incoming,
    results,
    back,
    out_w,
    projected,
    layer_out,
    layer_opposite,
    layer_merged,
    layer_side,
    residual,
    rows_buf,
    gate_up,
    down_w,
    partial,
    opposite_in,
    merged_out,
    side_in,
    row_sum,
    send2,
    opposite_in2,
    merged_out2,
    side_in2,
    local_sem,
    query_send_sem,
    query_recv_sem,
    back_send_sem,
    back_recv_sem,
    weight_send,
    weight_recv,
    send_sem,
    recv_sem,
):
    me = lax.axis_index("req")
    layer = lax.axis_index("mlp")
    core = lax.rem(me, 2)
    chip = me // 2
    row, col = chip // RING, lax.rem(chip, RING)
    rows, width = states_ref.shape
    head = query_gain_ref.shape[1]
    heads = query_w.shape[1] // head
    cols = heads * head
    hidden = gate_ref.shape[0]
    quarter = 2 * SUB
    score_scale = head ** (-0.5)
    f32, bf16 = jnp.float32, jnp.bfloat16

    def shifted(offset, sign=1):
        down, across, flip = offset // (2 * RING), (offset // 2) % RING, offset % 2
        if sign < 0:
            down, across = (RING - down) % RING, (RING - across) % RING
        row_at = lax.rem(row + down, RING)
        col_at = lax.rem(col + across, RING)
        core_at = 1 - core if flip else core
        return ((row_at * RING + col_at) * 2 + core_at, layer)

    right, left, sibling = shifted(2), shifted(2, -1), shifted(1)
    upper, lower = shifted(2 * RING), shifted(2 * RING, -1)
    above = (me, lax.rem(layer + 1, RING))
    below = (me, lax.rem(layer + RING - 1, RING))

    barrier = pltpu.get_barrier_semaphore()
    for offset in range(1, PEERS):
        pl.semaphore_signal(barrier, inc=1, device_id=shifted(offset), device_id_type=MESH_ID)
    for peer in (above, below):
        pl.semaphore_signal(barrier, inc=1, device_id=peer, device_id_type=MESH_ID)

    sources = (gate_ref, up_ref, down_ref)
    targets = (
        gate_up.at[pl.ds(0, hidden)],
        gate_up.at[pl.ds(2 * hidden, hidden)],
        down_w.at[pl.ds(0, hidden)],
    )
    far_targets = (
        gate_up.at[pl.ds(hidden, hidden)],
        gate_up.at[pl.ds(3 * hidden, hidden)],
        down_w.at[pl.ds(hidden, hidden)],
    )
    local = []
    for index, (src, dst) in enumerate(
        (
            (query_w_ref, query_w),
            (key_w_ref, key_w),
            (value_w_ref, value_w),
            (keys_ref, stored_keys),
            (values_ref, stored_values),
            (out_w_ref, out_w),
        )
        + tuple(zip(sources, targets))
    ):
        copy = pltpu.make_async_copy(src, dst, local_sem.at[index])
        copy.start()
        local.append(copy)

    def line(ref):
        return jnp.concatenate([ref[i : i + 1] for i in range(ref.shape[0])], axis=1)

    normalized = normed(states_ref[...].astype(f32), line(attn_gain_ref)).astype(bf16)

    def column(values):
        return jnp.transpose(jnp.broadcast_to(values, (128, rows)))[:, :1]

    prefix_row = prefix_ref[...].astype(f32)
    prefix_col = column(prefix_row)
    row_at = lax.broadcasted_iota(jnp.int32, (rows, rows), 0)
    col_at = lax.broadcasted_iota(jnp.int32, (rows, rows), 1)
    same = jnp.where(
        (prefix_col == prefix_row) & (((row_at >> 3) & 1) == ((col_at >> 3) & 1)), 1.0, 0.0
    )
    rank_col = jnp.sum(jnp.where(col_at < row_at, same, 0.0), axis=1, keepdims=True)
    rank_row = jnp.sum(jnp.where(row_at < col_at, same, 0.0), axis=0, keepdims=True)
    groups = owner_ref.shape[1]
    onehot = prefix_col == lax.broadcasted_iota(jnp.int32, (rows, groups), 1).astype(f32)
    owner_col = jnp.sum(jnp.where(onehot, owner_ref[...].astype(f32), 0.0), axis=1, keepdims=True)
    owner_row = jnp.transpose(jnp.broadcast_to(owner_col, (rows, 128)))[:1]

    def place(owner, rank):
        owner = owner.astype(jnp.int32)
        down = ((owner >> 3) - row) & 3
        across = (((owner >> 1) & 3) - col) & 3
        flip = ((owner & 1) - core) & 1
        return (down * 8 + across * 2 + flip) * CAP + rank.astype(jnp.int32)

    place_col = place(owner_col, rank_col)
    place_row = place(owner_row, rank_row)
    set_row = (lax.broadcasted_iota(jnp.int32, (1, rows), 1) >> 3) & 1

    def of_set(values, group):
        count, lanes = values.shape
        return values.reshape(count // 16, 2, 8, lanes)[:, group].reshape(count // 2, lanes)

    local[0].wait()
    raw = jnp.dot(normalized, query_w[...], preferred_element_type=f32)
    queries = [
        normed(raw[:, g * head : (g + 1) * head], query_gain_ref[...]).astype(bf16)
        for g in range(heads)
    ]
    query_rows = jnp.concatenate(queries, axis=1)
    pl.semaphore_wait(barrier, PEERS + 1)
    slot_at = lax.broadcasted_iota(jnp.int32, (PART * CAP, rows), 0)
    def send_queries(group):
        goal = jnp.where(set_row == group, place_row, -1)
        for part in range(PEERS // PART):
            placing = jnp.where(slot_at + part * PART * CAP == goal, 1.0, 0.0).astype(bf16)
            packed = jnp.dot(placing, query_rows, preferred_element_type=f32).astype(bf16)
            packed = packed.reshape(PART, CAP, cols)
            if part == 0:
                incoming[group, 0] = packed[0]
            outgoing[group, pl.ds(part * PART, PART)] = packed
            for offset in range(max(part * PART, 1), (part + 1) * PART):
                pltpu.make_async_remote_copy(
                    src_ref=outgoing.at[group, offset],
                    dst_ref=incoming.at[group, offset],
                    send_sem=query_send_sem.at[group],
                    recv_sem=query_recv_sem.at[group, part],
                    device_id=shifted(offset),
                    device_id_type=MESH_ID,
                ).start()

    send_queries(0)
    weight_copies = []
    for index, (src, dst) in enumerate(zip(sources, far_targets)):
        copy = pltpu.make_async_remote_copy(
            src_ref=src,
            dst_ref=dst,
            send_sem=weight_send.at[index],
            recv_sem=weight_recv.at[index],
            device_id=sibling,
            device_id_type=MESH_ID,
        )
        copy.start()
        weight_copies.append(copy)

    local[1].wait()
    local[2].wait()
    raw = jnp.dot(normalized, key_w[...], preferred_element_type=f32)
    keys = normed(raw, key_gain_ref[...]).astype(bf16)
    values = jnp.dot(normalized, value_w[...], preferred_element_type=f32).astype(bf16)
    segment_row = segment_ref[...].astype(f32)
    allowed = (column(segment_row) == segment_row) & (row_at >= col_at)

    def attend(query, key, value, mask):
        scores = (
            lax.dot_general(query, key, (((1,), (1,)), ((), ())), preferred_element_type=f32)
            * score_scale
        )
        if mask is not None:
            scores = jnp.where(mask, scores, -jnp.inf)
        row_max = jnp.max(scores, axis=-1, keepdims=True)
        powers = jnp.exp(scores - row_max)
        total = jnp.sum(powers, axis=-1, keepdims=True)
        weights = (powers / total).astype(bf16)
        mixed = jnp.dot(weights, value, preferred_element_type=f32)
        return mixed, row_max + jnp.log(total)

    suffix = [attend(query, keys, values, allowed) for query in queries]
    send_queries(1)

    def remote_blocks(buf, group, part):
        start = max(part * PART, 1)
        return buf.at[group, pl.ds(start, (part + 1) * PART - start)]

    def await_blocks(buf, group, part, sem):
        blocks = remote_blocks(buf, group, part)
        pltpu.make_async_copy(blocks, blocks, sem).wait()

    local[3].wait()
    local[4].wait()
    lanes = lax.broadcasted_iota(jnp.int32, (PART * CAP, 128), 1)
    def answer(group):
        for part in range(PEERS // PART):
            await_blocks(incoming, group, part, query_recv_sem.at[group, part])
            blocks = pl.ds(part * PART, PART)
            query = incoming[group, blocks].reshape(PART * CAP, cols)
            tail = jnp.zeros((PART * CAP, 128), f32)
            for g in range(heads):
                mixed, log_total = attend(
                    query[:, g * head : (g + 1) * head], stored_keys[...], stored_values[...], None
                )
                coarse = log_total.astype(bf16).astype(f32)
                tail = jnp.where(lanes == 2 * g, coarse, tail)
                tail = jnp.where(lanes == 2 * g + 1, log_total - coarse, tail)
                results[group, blocks, :, pl.ds(g * head, head)] = mixed.astype(bf16).reshape(
                    PART, CAP, head
                )
            results[group, blocks, :, pl.ds(cols, 128)] = tail.astype(bf16).reshape(
                PART, CAP, 128
            )

    def send_answers(group):
        for part in range(PEERS // PART):
            if part == 0:
                back[group, 0] = results[group, 0]
            for offset in range(max(part * PART, 1), (part + 1) * PART):
                pltpu.make_async_remote_copy(
                    src_ref=results.at[group, offset],
                    dst_ref=back.at[group, offset],
                    send_sem=back_send_sem.at[group],
                    recv_sem=back_recv_sem.at[group, part],
                    device_id=shifted(offset, -1),
                    device_id_type=MESH_ID,
                ).start()


    answer(0)
    send_answers(0)
    answer(1)
    blocks = results.at[0, pl.ds(1, PEERS - 1)]
    pltpu.make_async_copy(blocks, blocks, back_send_sem.at[0]).wait()
    send_answers(1)

    copies = []

    def send(src, dst, peer):
        index = len(copies)
        copy = pltpu.make_async_remote_copy(
            src_ref=src,
            dst_ref=dst,
            send_sem=send_sem.at[index],
            recv_sem=recv_sem.at[index],
            device_id=peer,
            device_id_type=MESH_ID,
        )
        copy.start()
        copies.append(copy)
        return copy

    def quarter_rows(ref, group, offset, start, size):
        at = lax.rem(layer + offset, RING) * SUB + start
        return ref.at[group, pl.ds(pl.multiple_of(at, HALF), size)]

    layer_opp, layer_plain, layer_far = {}, {}, {}

    def project(group):
        picked = jnp.zeros((rows // 2, cols + 128), f32)
        places = of_set(place_col, group)
        for part in range(PEERS // PART):
            await_blocks(back, group, part, back_recv_sem.at[group, part])
            slots = lax.broadcasted_iota(jnp.int32, (rows // 2, PART * CAP), 1)
            choosing = jnp.where(slots + part * PART * CAP == places, 1.0, 0.0).astype(bf16)
            block = back[group, pl.ds(part * PART, PART)].reshape(PART * CAP, cols + 128)
            picked = picked + jnp.dot(choosing, block, preferred_element_type=f32)
        attended = []
        for g in range(heads):
            mixed, log_total = suffix[g]
            at = cols + 2 * g
            prefix_lse = picked[:, at : at + 1] + picked[:, at + 1 : at + 2]
            blend = jax.nn.sigmoid(prefix_lse - of_set(log_total, group))
            attended.append(
                (
                    blend * picked[:, g * head : (g + 1) * head]
                    + (1.0 - blend) * of_set(mixed, group)
                ).astype(bf16)
            )
        out = jnp.dot(jnp.concatenate(attended, axis=1), out_w[...], preferred_element_type=f32)
        projected[group] = out
        layer_out[group] = out.astype(bf16)
        layer_opp[group] = (
            send(quarter_rows(layer_out, group, 2, 0, HALF), layer_opposite.at[0, group], above),
            send(quarter_rows(layer_out, group, 2, HALF, HALF), layer_opposite.at[1, group], below),
        )
        layer_plain[group] = (
            send(
                quarter_rows(layer_out, group, 1, HALF, HALF),
                layer_side.at[0, group, pl.ds(HALF, HALF)],
                above,
            ),
            send(
                quarter_rows(layer_out, group, 3, 0, HALF),
                layer_side.at[1, group, pl.ds(0, HALF)],
                below,
            ),
        )

    def merge_layers(group):
        layer_opp[group][0].wait_recv()
        layer_merged[0, group] = (
            quarter_rows(projected, group, 1, 0, HALF)[...] + layer_opposite[0, group].astype(f32)
        ).astype(bf16)
        a = send(layer_merged.at[0, group], layer_side.at[0, group, pl.ds(0, HALF)], above)
        layer_opp[group][1].wait_recv()
        layer_merged[1, group] = (
            quarter_rows(projected, group, 3, HALF, HALF)[...]
            + layer_opposite[1, group].astype(f32)
        ).astype(bf16)
        b = send(layer_merged.at[1, group], layer_side.at[1, group, pl.ds(HALF, HALF)], below)
        layer_far[group] = (a, b)

    first = ((right, left), (upper, lower))
    second = ((upper, lower), (right, left))
    step1, step2, across, relays = {}, {}, {}, {}

    def slot(group, chunk, sub, start=0, size=SUB):
        return rows_buf.at[chunk, pl.ds(group * SPAN + sub * SUB + start, size)]

    def send_across(group, sub):
        plus, minus = second[group]
        across[group, sub] = (
            send(slot(group, 0, sub), slot(group, 3, sub), plus),
            send(slot(group, 0, sub), slot(group, 1, sub), minus),
        )

    def relay_across(group, sub):
        plus, minus = second[group]
        across[group, sub][0].wait_recv()
        a = send(slot(group, 3, sub, 0, HALF), slot(group, 2, sub, 0, HALF), plus)
        across[group, sub][1].wait_recv()
        b = send(slot(group, 1, sub, HALF, HALF), slot(group, 2, sub, HALF, HALF), minus)
        relays[group, sub] = (a, b)

    def enter(group):
        for copy in layer_plain[group] + layer_far[group]:
            copy.wait_recv()
        total = (
            quarter_rows(projected, group, 0, 0, SUB)[...]
            + layer_side[0, group].astype(f32)
            + layer_side[1, group].astype(f32)
        )
        own = states_ref[pl.ds(pl.multiple_of(layer * quarter, quarter), quarter)].astype(f32)
        after = of_set(own, group) + normed(total, line(post_gain_ref))
        residual[group] = after
        rows_buf[0, pl.ds(group * SPAN, SUB)] = normed(after, line(ffw_gain_ref)).astype(bf16)
        plus, minus = first[group]
        step1[group] = (
            send(slot(group, 0, 0), slot(group, 0, 3), plus),
            send(slot(group, 0, 0), slot(group, 0, 1), minus),
        )
        send_across(group, 0)

    def spread(group):
        plus, minus = first[group]
        step1[group][0].wait_recv()
        a = send(slot(group, 0, 3, 0, HALF), slot(group, 0, 2, 0, HALF), plus)
        step1[group][1].wait_recv()
        b = send(slot(group, 0, 1, HALF, HALF), slot(group, 0, 2, HALF, HALF), minus)
        step2[group] = (a, b)
        send_across(group, 1)
        send_across(group, 3)

    def finish_spread(group):
        for copy in step2[group]:
            copy.wait_recv()
        send_across(group, 2)

    def compute(chunk, start, size):
        span = pl.ds(start, size)
        both = lax.dot_general(
            rows_buf[chunk, span],
            gate_up[...],
            (((1,), (1,)), ((), ())),
            preferred_element_type=f32,
        )
        gate = both[:, : 2 * hidden]
        act = (jax.nn.gelu(gate, approximate=True) * both[:, 2 * hidden :]).astype(bf16)
        partial[chunk, span] = jnp.dot(act, down_w[...], preferred_element_type=f32).astype(bf16)

    local[5].wait()
    project(0)
    merge_layers(0)
    enter(0)
    project(1)
    merge_layers(1)
    spread(0)
    relay_across(0, 0)
    enter(1)
    finish_spread(0)
    spread(1)
    relay_across(0, 1)
    relay_across(0, 3)
    relay_across(1, 0)
    finish_spread(1)
    for copy in local[6:]:
        copy.wait()
    for copy in weight_copies:
        copy.wait_recv()
    relay_across(0, 2)
    relay_across(1, 1)
    relay_across(1, 3)
    compute(0, 0, 2 * SPAN)
    relay_across(1, 2)
    compute(1, 0, 2 * SPAN)
    compute(3, 0, 2 * SPAN)

    opposite, plain, merged, last = {}, {}, {}, {}

    def piece(group, chunk, sub, start):
        return partial.at[chunk, pl.ds(group * SPAN + sub * SUB + start, HALF)]

    def side(group, which, sub, start):
        return side_in.at[which, group, sub, pl.ds(start, HALF)]

    def send_opposite(group):
        plus, minus = second[group]
        for sub in ORDER:
            opposite[group, sub] = (
                send(piece(group, 2, sub, 0), opposite_in.at[0, group, sub], plus),
                send(piece(group, 2, sub, HALF), opposite_in.at[1, group, sub], minus),
            )

    def send_plain(group):
        plus, minus = second[group]
        for sub in ORDER:
            plain[group, sub] = (
                send(piece(group, 1, sub, HALF), side(group, 0, sub, HALF), plus),
                send(piece(group, 3, sub, 0), side(group, 1, sub, 0), minus),
            )

    def merge(group, sub):
        plus, minus = second[group]
        opposite[group, sub][0].wait_recv()
        merged_out[0, group, sub] = (
            piece(group, 1, sub, 0)[...].astype(f32) + opposite_in[0, group, sub].astype(f32)
        ).astype(bf16)
        a = send(merged_out.at[0, group, sub], side(group, 0, sub, 0), plus)
        opposite[group, sub][1].wait_recv()
        merged_out[1, group, sub] = (
            piece(group, 3, sub, HALF)[...].astype(f32) + opposite_in[1, group, sub].astype(f32)
        ).astype(bf16)
        b = send(merged_out.at[1, group, sub], side(group, 1, sub, HALF), minus)
        merged[group, sub] = (a, b)

    def summed(group, sub):
        for copy in plain[group, sub] + merged[group, sub]:
            copy.wait_recv()
        return (
            partial[0, pl.ds(group * SPAN + sub * SUB, SUB)].astype(f32)
            + side_in[0, group, sub].astype(f32)
            + side_in[1, group, sub].astype(f32)
        )

    def turn_opposite(group):
        plus, minus = first[group]
        send2[group, 2] = summed(group, 2).astype(bf16)
        last[group, 0] = send(
            send2.at[group, 2, pl.ds(0, HALF)], opposite_in2.at[group, 0], plus
        )
        last[group, 1] = send(
            send2.at[group, 2, pl.ds(HALF, HALF)], opposite_in2.at[group, 1], minus
        )

    def turn_side(group, which):
        sub = (1, 3)[which]
        start = (HALF, 0)[which]
        row_sum[group, which] = summed(group, sub)
        send2[group, sub] = row_sum[group, which].astype(bf16)
        last[group, 2 + which] = send(
            send2.at[group, sub, pl.ds(start, HALF)],
            side_in2.at[group, which, pl.ds(start, HALF)],
            first[group][which],
        )

    def turn_merge(group, which):
        start = (0, HALF)[which]
        last[group, which].wait_recv()
        merged_out2[group, which] = (
            row_sum[group, which, pl.ds(start, HALF)] + opposite_in2[group, which].astype(f32)
        ).astype(bf16)
        last[group, 4 + which] = send(
            merged_out2.at[group, which],
            side_in2.at[group, which, pl.ds(start, HALF)],
            first[group][which],
        )

    def finish(group):
        own = summed(group, 0)
        for index in (2, 3, 4, 5):
            last[group, index].wait_recv()
        total = own + side_in2[group, 0].astype(f32) + side_in2[group, 1].astype(f32)
        return residual[group] + normed(total, line(last_gain_ref))

    send_plain(0)
    for sub in range(RING):
        relays[0, sub][0].wait_recv()
        relays[0, sub][1].wait_recv()
    compute(2, 0, SPAN)
    send_opposite(0)
    send_plain(1)
    for sub in range(RING):
        relays[1, sub][0].wait_recv()
        relays[1, sub][1].wait_recv()
    compute(2, SPAN, SPAN)
    send_opposite(1)
    for sub in ORDER:
        merge(0, sub)
        merge(1, sub)
    for group in range(2):
        turn_opposite(group)
    for group in range(2):
        turn_side(group, 0)
        turn_side(group, 1)
    for group in range(2):
        turn_merge(group, 0)
        turn_merge(group, 1)
    ends = [finish(group).reshape(RING, 1, 8, width) for group in range(2)]
    out_ref[...] = jnp.concatenate(ends, axis=1).reshape(quarter, width).astype(out_ref.dtype)

    for group in range(2):
        blocks = outgoing.at[group, pl.ds(1, PEERS - 1)]
        pltpu.make_async_copy(blocks, blocks, query_send_sem.at[group]).wait()
    blocks = results.at[1, pl.ds(1, PEERS - 1)]
    pltpu.make_async_copy(blocks, blocks, back_send_sem.at[1]).wait()
    for copy in copies + weight_copies:
        copy.wait_send()


def body(
    states,
    attn_gain,
    query_matrix,
    key_matrix,
    value_matrix,
    query_gain,
    key_gain,
    out_weight,
    post_gain,
    ffw_gain,
    gate_weight,
    up_weight,
    down_weight,
    post_ffw_gain,
    prefix_key_cache,
    prefix_value_cache,
    segment,
    prefix_id,
    owner_map,
):
    rows, width = states.shape
    cols = query_matrix.shape[1]
    hidden = gate_weight.shape[1]
    keys, values = prefix_key_cache[0], prefix_value_cache[0]
    vmem = pl.BlockSpec(memory_space=pltpu.VMEM)
    hbm = pl.BlockSpec(memory_space=pl.ANY)
    f32, bf16 = jnp.float32, jnp.bfloat16
    links = 112
    dma = pltpu.SemaphoreType.DMA
    return pl.pallas_call(
        layer_kernel,
        out_shape=jax.ShapeDtypeStruct((2 * SUB, width), bf16),
        in_specs=[vmem] * 10 + [hbm] * 9,
        out_specs=vmem,
        scratch_shapes=[
            pltpu.VMEM(query_matrix.shape, bf16),
            pltpu.VMEM(key_matrix.shape, bf16),
            pltpu.VMEM(value_matrix.shape, bf16),
            pltpu.VMEM(keys.shape, bf16),
            pltpu.VMEM(values.shape, bf16),
            pltpu.VMEM((2, PEERS, CAP, cols), bf16),
            pltpu.VMEM((2, PEERS, CAP, cols), bf16),
            pltpu.VMEM((2, PEERS, CAP, cols + 128), bf16),
            pltpu.VMEM((2, PEERS, CAP, cols + 128), bf16),
            pltpu.VMEM(out_weight.shape, bf16),
            pltpu.VMEM((2, SPAN, width), f32),
            pltpu.VMEM((2, SPAN, width), bf16),
            pltpu.VMEM((2, 2, HALF, width), bf16),
            pltpu.VMEM((2, 2, HALF, width), bf16),
            pltpu.VMEM((2, 2, SUB, width), bf16),
            pltpu.VMEM((2, SUB, width), f32),
            pltpu.VMEM((RING, 2 * SPAN, width), bf16),
            pltpu.VMEM((4 * hidden, width), bf16),
            pltpu.VMEM((2 * hidden, width), bf16),
            pltpu.VMEM((RING, 2 * SPAN, width), bf16),
            pltpu.VMEM((2, 2, RING, HALF, width), bf16),
            pltpu.VMEM((2, 2, RING, HALF, width), bf16),
            pltpu.VMEM((2, 2, RING, SUB, width), bf16),
            pltpu.VMEM((2, 2, SUB, width), f32),
            pltpu.VMEM((2, RING, SUB, width), bf16),
            pltpu.VMEM((2, 2, HALF, width), bf16),
            pltpu.VMEM((2, 2, HALF, width), bf16),
            pltpu.VMEM((2, 2, SUB, width), bf16),
            dma((9,)),
            dma((2,)),
            dma((2, 2)),
            dma((2,)),
            dma((2, 2)),
            dma((3,)),
            dma((3,)),
            dma((links,)),
            dma((links,)),
        ],
        compiler_params=pltpu.CompilerParams(
            collective_id=0, has_side_effects=True, vmem_limit_bytes=60 << 20
        ),
        name="layer",
    )(
        states,
        attn_gain.reshape(-1, 128),
        query_gain[None],
        key_gain[None],
        segment[None],
        prefix_id[None],
        owner_map[None],
        post_gain.reshape(-1, 128),
        ffw_gain.reshape(-1, 128),
        post_ffw_gain.reshape(-1, 128),
        query_matrix,
        key_matrix,
        value_matrix,
        keys,
        values,
        out_weight,
        gate_weight.T,
        up_weight.T,
        down_weight,
    )


def solution(mesh):
    return jax.shard_map(
        body,
        mesh=mesh,
        in_specs=(
            P("req", None),
            P(),
            P(None, "mlp"),
            P(None, "mlp"),
            P(None, "mlp"),
            P(),
            P(),
            P("mlp", None),
            P(),
            P(),
            P(None, "req"),
            P(None, "req"),
            P("req", None),
            P(),
            P("req", None, "mlp"),
            P("req", None, "mlp"),
            P("req"),
            P("req"),
            P(),
        ),
        out_specs=P(("req", "mlp"), None),
        check_vma=False,
    )
```

```python
import jax
import jax.numpy as jnp
from jax import lax
from jax.experimental import pallas as pl
from jax.experimental.pallas import tpu as pltpu
from jax.sharding import PartitionSpec as P

EPS = 1e-06

MESH_ID = pl.DeviceIdType.MESH
RING = 4
SUB = 32
HALF = 16
CAP = 16
PEERS = 2 * RING * RING
PART = 16
SPAN = RING * SUB
ORDER = (2, 1, 3, 0)


def normed(values_in, gain_vec):
    return (
        values_in
        * lax.rsqrt(jnp.mean(values_in * values_in, axis=-1, keepdims=True) + EPS)
        * gain_vec
    )


def layer_kernel(
    states_ref,
    attn_gain_ref,
    query_gain_ref,
    key_gain_ref,
    segment_ref,
    prefix_ref,
    owner_ref,
    post_gain_ref,
    ffw_gain_ref,
    last_gain_ref,
    query_w_ref,
    key_w_ref,
    value_w_ref,
    keys_ref,
    values_ref,
    out_w_ref,
    gate_ref,
    up_ref,
    down_ref,
    out_ref,
    query_w,
    key_w,
    value_w,
    stored_keys,
    stored_values,
    outgoing,
    incoming,
    results,
    back,
    log_out,
    log_back,
    out_w,
    projected,
    layer_out,
    layer_opposite,
    layer_merged,
    layer_side,
    residual,
    rows_buf,
    gate_up,
    down_w,
    partial,
    opposite_in,
    merged_out,
    side_in,
    row_sum,
    send2,
    opposite_in2,
    merged_out2,
    side_in2,
    local_sem,
    query_send_sem,
    query_recv_sem,
    back_send_sem,
    back_recv_sem,
    log_send_sem,
    log_recv_sem,
    weight_send,
    weight_recv,
    send_sem,
    recv_sem,
):
    me = lax.axis_index("req")
    layer = lax.axis_index("mlp")
    core = lax.rem(me, 2)
    chip = me // 2
    row, col = chip // RING, lax.rem(chip, RING)
    rows, width = states_ref.shape
    head = query_gain_ref.shape[1]
    heads = query_w.shape[1] // head
    cols = heads * head
    hidden = gate_ref.shape[0]
    quarter = 2 * SUB
    score_scale = head ** (-0.5)
    f32, bf16 = jnp.float32, jnp.bfloat16

    def shifted(offset, sign=1):
        down, across, flip = offset // (2 * RING), (offset // 2) % RING, offset % 2
        if sign < 0:
            down, across = (RING - down) % RING, (RING - across) % RING
        row_at = lax.rem(row + down, RING)
        col_at = lax.rem(col + across, RING)
        core_at = 1 - core if flip else core
        return ((row_at * RING + col_at) * 2 + core_at, layer)

    right, left, sibling = shifted(2), shifted(2, -1), shifted(1)
    upper, lower = shifted(2 * RING), shifted(2 * RING, -1)
    above = (me, lax.rem(layer + 1, RING))
    below = (me, lax.rem(layer + RING - 1, RING))

    barrier = pltpu.get_barrier_semaphore()
    for offset in range(1, PEERS):
        pl.semaphore_signal(barrier, inc=1, device_id=shifted(offset), device_id_type=MESH_ID)
    for peer in (above, below):
        pl.semaphore_signal(barrier, inc=1, device_id=peer, device_id_type=MESH_ID)

    sources = (gate_ref, up_ref, down_ref)
    targets = (
        gate_up.at[pl.ds(0, hidden)],
        gate_up.at[pl.ds(2 * hidden, hidden)],
        down_w.at[pl.ds(0, hidden)],
    )
    far_targets = (
        gate_up.at[pl.ds(hidden, hidden)],
        gate_up.at[pl.ds(3 * hidden, hidden)],
        down_w.at[pl.ds(hidden, hidden)],
    )
    local = []
    for index, (src, dst) in enumerate(
        (
            (query_w_ref, query_w),
            (key_w_ref, key_w),
            (value_w_ref, value_w),
            (keys_ref, stored_keys),
            (values_ref, stored_values),
            (out_w_ref, out_w),
        )
        + tuple(zip(sources, targets))
    ):
        copy = pltpu.make_async_copy(src, dst, local_sem.at[index])
        copy.start()
        local.append(copy)

    def line(ref):
        return jnp.concatenate([ref[i : i + 1] for i in range(ref.shape[0])], axis=1)

    normalized = normed(states_ref[...].astype(f32), line(attn_gain_ref)).astype(bf16)

    def column(values):
        return jnp.transpose(jnp.broadcast_to(values, (128, rows)))[:, :1]

    prefix_row = prefix_ref[...].astype(f32)
    prefix_col = column(prefix_row)
    row_at = lax.broadcasted_iota(jnp.int32, (rows, rows), 0)
    col_at = lax.broadcasted_iota(jnp.int32, (rows, rows), 1)
    same = jnp.where(
        (prefix_col == prefix_row) & (((row_at >> 3) & 1) == ((col_at >> 3) & 1)), 1.0, 0.0
    )
    rank_col = jnp.sum(jnp.where(col_at < row_at, same, 0.0), axis=1, keepdims=True)
    rank_row = jnp.sum(jnp.where(row_at < col_at, same, 0.0), axis=0, keepdims=True)
    groups = owner_ref.shape[1]
    onehot = prefix_col == lax.broadcasted_iota(jnp.int32, (rows, groups), 1).astype(f32)
    owner_col = jnp.sum(jnp.where(onehot, owner_ref[...].astype(f32), 0.0), axis=1, keepdims=True)
    owner_row = jnp.transpose(jnp.broadcast_to(owner_col, (rows, 128)))[:1]

    def place(owner, rank):
        owner = owner.astype(jnp.int32)
        down = ((owner >> 3) - row) & 3
        across = (((owner >> 1) & 3) - col) & 3
        flip = ((owner & 1) - core) & 1
        return (down * 8 + across * 2 + flip) * CAP + rank.astype(jnp.int32)

    place_col = place(owner_col, rank_col)
    place_row = place(owner_row, rank_row)
    set_row = (lax.broadcasted_iota(jnp.int32, (1, rows), 1) >> 3) & 1

    def of_set(values, group):
        count, lanes = values.shape
        return values.reshape(count // 16, 2, 8, lanes)[:, group].reshape(count // 2, lanes)

    local[0].wait()
    raw = jnp.dot(normalized, query_w[...], preferred_element_type=f32)
    queries = [
        normed(raw[:, g * head : (g + 1) * head], query_gain_ref[...]).astype(bf16)
        for g in range(heads)
    ]
    query_rows = jnp.concatenate(queries, axis=1)
    pl.semaphore_wait(barrier, PEERS + 1)
    slot_at = lax.broadcasted_iota(jnp.int32, (PART * CAP, rows), 0)
    def send_queries(group):
        goal = jnp.where(set_row == group, place_row, -1)
        for part in range(PEERS // PART):
            placing = jnp.where(slot_at + part * PART * CAP == goal, 1.0, 0.0).astype(bf16)
            packed = jnp.dot(placing, query_rows, preferred_element_type=f32).astype(bf16)
            packed = packed.reshape(PART, CAP, cols)
            if part == 0:
                incoming[group, 0] = packed[0]
            outgoing[group, pl.ds(part * PART, PART)] = packed
            for offset in range(max(part * PART, 1), (part + 1) * PART):
                pltpu.make_async_remote_copy(
                    src_ref=outgoing.at[group, offset],
                    dst_ref=incoming.at[group, offset],
                    send_sem=query_send_sem.at[group],
                    recv_sem=query_recv_sem.at[group, part],
                    device_id=shifted(offset),
                    device_id_type=MESH_ID,
                ).start()

    send_queries(0)
    weight_copies = []
    for index, (src, dst) in enumerate(zip(sources, far_targets)):
        copy = pltpu.make_async_remote_copy(
            src_ref=src,
            dst_ref=dst,
            send_sem=weight_send.at[index],
            recv_sem=weight_recv.at[index],
            device_id=sibling,
            device_id_type=MESH_ID,
        )
        copy.start()
        weight_copies.append(copy)

    local[1].wait()
    local[2].wait()
    raw = jnp.dot(normalized, key_w[...], preferred_element_type=f32)
    keys = normed(raw, key_gain_ref[...]).astype(bf16)
    values = jnp.dot(normalized, value_w[...], preferred_element_type=f32).astype(bf16)
    segment_row = segment_ref[...].astype(f32)
    allowed = (column(segment_row) == segment_row) & (row_at >= col_at)

    def attend(query, key, value, mask):
        scores = (
            lax.dot_general(query, key, (((1,), (1,)), ((), ())), preferred_element_type=f32)
            * score_scale
        )
        if mask is not None:
            scores = jnp.where(mask, scores, -jnp.inf)
        row_max = jnp.max(scores, axis=-1, keepdims=True)
        powers = jnp.exp(scores - row_max)
        total = jnp.sum(powers, axis=-1, keepdims=True)
        weights = (powers / total).astype(bf16)
        mixed = jnp.dot(weights, value, preferred_element_type=f32)
        return mixed, row_max + jnp.log(total)

    suffix = [attend(query, keys, values, allowed) for query in queries]
    send_queries(1)

    def remote_blocks(buf, group, part):
        start = max(part * PART, 1)
        return buf.at[group, pl.ds(start, (part + 1) * PART - start)]

    def await_blocks(buf, group, part, sem):
        blocks = remote_blocks(buf, group, part)
        pltpu.make_async_copy(blocks, blocks, sem).wait()

    local[3].wait()
    local[4].wait()
    lanes = lax.broadcasted_iota(jnp.int32, (PART * CAP, 128), 1)
    slot_of = lax.broadcasted_iota(jnp.int32, (PART * CAP, 128), 0) & (CAP - 1)
    def answer(group):
        for part in range(PEERS // PART):
            await_blocks(incoming, group, part, query_recv_sem.at[group, part])
            blocks = pl.ds(part * PART, PART)
            query = incoming[group, blocks].reshape(PART * CAP, cols)
            totals = jnp.zeros((PART * CAP, 128), f32)
            for g in range(heads):
                mixed, log_total = attend(
                    query[:, g * head : (g + 1) * head], stored_keys[...], stored_values[...], None
                )
                totals = jnp.where(lanes == CAP * g + slot_of, log_total, totals)
                results[group, blocks, :, pl.ds(g * head, head)] = mixed.astype(bf16).reshape(
                    PART, CAP, head
                )
            log_out[group, blocks] = jnp.sum(
                totals.reshape(PART, CAP, 128), axis=1, keepdims=True
            )

    def send_answers(group):
        for part in range(PEERS // PART):
            if part == 0:
                back[group, 0] = results[group, 0]
                log_back[group, 0] = log_out[group, 0]
            for offset in range(max(part * PART, 1), (part + 1) * PART):
                pltpu.make_async_remote_copy(
                    src_ref=results.at[group, offset],
                    dst_ref=back.at[group, offset],
                    send_sem=back_send_sem.at[group],
                    recv_sem=back_recv_sem.at[group, part],
                    device_id=shifted(offset, -1),
                    device_id_type=MESH_ID,
                ).start()
            for offset in range(max(part * PART, 1), (part + 1) * PART):
                pltpu.make_async_remote_copy(
                    src_ref=log_out.at[group, offset],
                    dst_ref=log_back.at[group, offset],
                    send_sem=log_send_sem.at[group],
                    recv_sem=log_recv_sem.at[group, part],
                    device_id=shifted(offset, -1),
                    device_id_type=MESH_ID,
                ).start()

    answer(0)
    send_answers(0)
    answer(1)
    blocks = results.at[0, pl.ds(1, PEERS - 1)]
    pltpu.make_async_copy(blocks, blocks, back_send_sem.at[0]).wait()
    send_answers(1)

    copies = []

    def send(src, dst, peer):
        index = len(copies)
        copy = pltpu.make_async_remote_copy(
            src_ref=src,
            dst_ref=dst,
            send_sem=send_sem.at[index],
            recv_sem=recv_sem.at[index],
            device_id=peer,
            device_id_type=MESH_ID,
        )
        copy.start()
        copies.append(copy)
        return copy

    def quarter_rows(ref, group, offset, start, size):
        at = lax.rem(layer + offset, RING) * SUB + start
        return ref.at[group, pl.ds(pl.multiple_of(at, HALF), size)]

    layer_opp, layer_plain, layer_far = {}, {}, {}

    def project(group):
        picked = jnp.zeros((rows // 2, cols), f32)
        places = of_set(place_col, group)
        for part in range(PEERS // PART):
            await_blocks(back, group, part, back_recv_sem.at[group, part])
            slots = lax.broadcasted_iota(jnp.int32, (rows // 2, PART * CAP), 1)
            choosing = jnp.where(slots + part * PART * CAP == places, 1.0, 0.0).astype(bf16)
            block = back[group, pl.ds(part * PART, PART)].reshape(PART * CAP, cols)
            picked = picked + jnp.dot(choosing, block, preferred_element_type=f32)
            await_blocks(log_back, group, part, log_recv_sem.at[group, part])
        peer_at = lax.broadcasted_iota(jnp.int32, (rows // 2, PEERS), 1)
        totals = jnp.dot(
            jnp.where(peer_at == places >> 4, 1.0, 0.0),
            log_back[group].reshape(PEERS, 128),
            precision=lax.Precision.HIGHEST,
            preferred_element_type=f32,
        )
        lane_at = lax.broadcasted_iota(jnp.int32, (rows // 2, 128), 1)
        attended = []
        for g in range(heads):
            mixed, log_total = suffix[g]
            prefix_lse = jnp.sum(
                jnp.where(lane_at == CAP * g + (places & (CAP - 1)), totals, 0.0),
                axis=1,
                keepdims=True,
            )
            blend = jax.nn.sigmoid(prefix_lse - of_set(log_total, group))
            attended.append(
                (
                    blend * picked[:, g * head : (g + 1) * head]
                    + (1.0 - blend) * of_set(mixed, group)
                ).astype(bf16)
            )
        out = jnp.dot(jnp.concatenate(attended, axis=1), out_w[...], preferred_element_type=f32)
        projected[group] = out
        layer_out[group] = out.astype(bf16)
        layer_opp[group] = (
            send(quarter_rows(layer_out, group, 2, 0, HALF), layer_opposite.at[0, group], above),
            send(quarter_rows(layer_out, group, 2, HALF, HALF), layer_opposite.at[1, group], below),
        )
        layer_plain[group] = (
            send(
                quarter_rows(layer_out, group, 1, HALF, HALF),
                layer_side.at[0, group, pl.ds(HALF, HALF)],
                above,
            ),
            send(
                quarter_rows(layer_out, group, 3, 0, HALF),
                layer_side.at[1, group, pl.ds(0, HALF)],
                below,
            ),
        )

    def merge_layers(group):
        layer_opp[group][0].wait_recv()
        layer_merged[0, group] = (
            quarter_rows(projected, group, 1, 0, HALF)[...] + layer_opposite[0, group].astype(f32)
        ).astype(bf16)
        a = send(layer_merged.at[0, group], layer_side.at[0, group, pl.ds(0, HALF)], above)
        layer_opp[group][1].wait_recv()
        layer_merged[1, group] = (
            quarter_rows(projected, group, 3, HALF, HALF)[...]
            + layer_opposite[1, group].astype(f32)
        ).astype(bf16)
        b = send(layer_merged.at[1, group], layer_side.at[1, group, pl.ds(HALF, HALF)], below)
        layer_far[group] = (a, b)

    first = ((right, left), (upper, lower))
    second = ((upper, lower), (right, left))
    step1, step2, across, relays = {}, {}, {}, {}

    def slot(group, chunk, sub, start=0, size=SUB):
        return rows_buf.at[chunk, pl.ds(group * SPAN + sub * SUB + start, size)]

    def send_across(group, sub):
        plus, minus = second[group]
        across[group, sub] = (
            send(slot(group, 0, sub), slot(group, 3, sub), plus),
            send(slot(group, 0, sub), slot(group, 1, sub), minus),
        )

    def relay_across(group, sub):
        plus, minus = second[group]
        across[group, sub][0].wait_recv()
        a = send(slot(group, 3, sub, 0, HALF), slot(group, 2, sub, 0, HALF), plus)
        across[group, sub][1].wait_recv()
        b = send(slot(group, 1, sub, HALF, HALF), slot(group, 2, sub, HALF, HALF), minus)
        relays[group, sub] = (a, b)

    def enter(group):
        for copy in layer_plain[group] + layer_far[group]:
            copy.wait_recv()
        total = (
            quarter_rows(projected, group, 0, 0, SUB)[...]
            + layer_side[0, group].astype(f32)
            + layer_side[1, group].astype(f32)
        )
        own = states_ref[pl.ds(pl.multiple_of(layer * quarter, quarter), quarter)].astype(f32)
        after = of_set(own, group) + normed(total, line(post_gain_ref))
        residual[group] = after
        rows_buf[0, pl.ds(group * SPAN, SUB)] = normed(after, line(ffw_gain_ref)).astype(bf16)
        plus, minus = first[group]
        step1[group] = (
            send(slot(group, 0, 0), slot(group, 0, 3), plus),
            send(slot(group, 0, 0), slot(group, 0, 1), minus),
        )
        send_across(group, 0)

    def spread(group):
        plus, minus = first[group]
        step1[group][0].wait_recv()
        a = send(slot(group, 0, 3, 0, HALF), slot(group, 0, 2, 0, HALF), plus)
        step1[group][1].wait_recv()
        b = send(slot(group, 0, 1, HALF, HALF), slot(group, 0, 2, HALF, HALF), minus)
        step2[group] = (a, b)
        send_across(group, 1)
        send_across(group, 3)

    def finish_spread(group):
        for copy in step2[group]:
            copy.wait_recv()
        send_across(group, 2)

    def compute(chunk, start, size):
        span = pl.ds(start, size)
        both = lax.dot_general(
            rows_buf[chunk, span],
            gate_up[...],
            (((1,), (1,)), ((), ())),
            preferred_element_type=f32,
        )
        gate = both[:, : 2 * hidden]
        act = (jax.nn.gelu(gate, approximate=True) * both[:, 2 * hidden :]).astype(bf16)
        partial[chunk, span] = jnp.dot(act, down_w[...], preferred_element_type=f32).astype(bf16)

    local[5].wait()
    project(0)
    merge_layers(0)
    enter(0)
    project(1)
    merge_layers(1)
    spread(0)
    relay_across(0, 0)
    enter(1)
    finish_spread(0)
    spread(1)
    relay_across(0, 1)
    relay_across(0, 3)
    relay_across(1, 0)
    finish_spread(1)
    for copy in local[6:]:
        copy.wait()
    for copy in weight_copies:
        copy.wait_recv()
    relay_across(0, 2)
    relay_across(1, 1)
    relay_across(1, 3)
    compute(0, 0, 2 * SPAN)
    relay_across(1, 2)
    compute(1, 0, 2 * SPAN)
    compute(3, 0, 2 * SPAN)

    opposite, plain, merged, last = {}, {}, {}, {}

    def piece(group, chunk, sub, start):
        return partial.at[chunk, pl.ds(group * SPAN + sub * SUB + start, HALF)]

    def side(group, which, sub, start):
        return side_in.at[which, group, sub, pl.ds(start, HALF)]

    def send_opposite(group):
        plus, minus = second[group]
        for sub in ORDER:
            opposite[group, sub] = (
                send(piece(group, 2, sub, 0), opposite_in.at[0, group, sub], plus),
                send(piece(group, 2, sub, HALF), opposite_in.at[1, group, sub], minus),
            )

    def send_plain(group):
        plus, minus = second[group]
        for sub in ORDER:
            plain[group, sub] = (
                send(piece(group, 1, sub, HALF), side(group, 0, sub, HALF), plus),
                send(piece(group, 3, sub, 0), side(group, 1, sub, 0), minus),
            )

    def merge(group, sub):
        plus, minus = second[group]
        opposite[group, sub][0].wait_recv()
        merged_out[0, group, sub] = (
            piece(group, 1, sub, 0)[...].astype(f32) + opposite_in[0, group, sub].astype(f32)
        ).astype(bf16)
        a = send(merged_out.at[0, group, sub], side(group, 0, sub, 0), plus)
        opposite[group, sub][1].wait_recv()
        merged_out[1, group, sub] = (
            piece(group, 3, sub, HALF)[...].astype(f32) + opposite_in[1, group, sub].astype(f32)
        ).astype(bf16)
        b = send(merged_out.at[1, group, sub], side(group, 1, sub, HALF), minus)
        merged[group, sub] = (a, b)

    def summed(group, sub):
        for copy in plain[group, sub] + merged[group, sub]:
            copy.wait_recv()
        return (
            partial[0, pl.ds(group * SPAN + sub * SUB, SUB)].astype(f32)
            + side_in[0, group, sub].astype(f32)
            + side_in[1, group, sub].astype(f32)
        )

    def turn_opposite(group):
        plus, minus = first[group]
        send2[group, 2] = summed(group, 2).astype(bf16)
        last[group, 0] = send(
            send2.at[group, 2, pl.ds(0, HALF)], opposite_in2.at[group, 0], plus
        )
        last[group, 1] = send(
            send2.at[group, 2, pl.ds(HALF, HALF)], opposite_in2.at[group, 1], minus
        )

    def turn_side(group, which):
        sub = (1, 3)[which]
        start = (HALF, 0)[which]
        row_sum[group, which] = summed(group, sub)
        send2[group, sub] = row_sum[group, which].astype(bf16)
        last[group, 2 + which] = send(
            send2.at[group, sub, pl.ds(start, HALF)],
            side_in2.at[group, which, pl.ds(start, HALF)],
            first[group][which],
        )

    def turn_merge(group, which):
        start = (0, HALF)[which]
        last[group, which].wait_recv()
        merged_out2[group, which] = (
            row_sum[group, which, pl.ds(start, HALF)] + opposite_in2[group, which].astype(f32)
        ).astype(bf16)
        last[group, 4 + which] = send(
            merged_out2.at[group, which],
            side_in2.at[group, which, pl.ds(start, HALF)],
            first[group][which],
        )

    def finish(group):
        own = summed(group, 0)
        for index in (2, 3, 4, 5):
            last[group, index].wait_recv()
        total = own + side_in2[group, 0].astype(f32) + side_in2[group, 1].astype(f32)
        return residual[group] + normed(total, line(last_gain_ref))

    for group in range(2):
        send_plain(group)
    for pair in relays.values():
        pair[0].wait_recv()
        pair[1].wait_recv()
    compute(2, 0, 2 * SPAN)
    for group in range(2):
        send_opposite(group)
    for sub in ORDER:
        merge(0, sub)
        merge(1, sub)
    for group in range(2):
        turn_opposite(group)
    for group in range(2):
        turn_side(group, 0)
        turn_side(group, 1)
    for group in range(2):
        turn_merge(group, 0)
        turn_merge(group, 1)
    ends = [finish(group).reshape(RING, 1, 8, width) for group in range(2)]
    out_ref[...] = jnp.concatenate(ends, axis=1).reshape(quarter, width).astype(out_ref.dtype)

    for group in range(2):
        for buf, sem in ((outgoing, query_send_sem), (log_out, log_send_sem)):
            blocks = buf.at[group, pl.ds(1, PEERS - 1)]
            pltpu.make_async_copy(blocks, blocks, sem.at[group]).wait()
    blocks = results.at[1, pl.ds(1, PEERS - 1)]
    pltpu.make_async_copy(blocks, blocks, back_send_sem.at[1]).wait()
    for copy in copies + weight_copies:
        copy.wait_send()


def body(
    states,
    attn_gain,
    query_matrix,
    key_matrix,
    value_matrix,
    query_gain,
    key_gain,
    out_weight,
    post_gain,
    ffw_gain,
    gate_weight,
    up_weight,
    down_weight,
    post_ffw_gain,
    prefix_key_cache,
    prefix_value_cache,
    segment,
    prefix_id,
    owner_map,
):
    rows, width = states.shape
    cols = query_matrix.shape[1]
    hidden = gate_weight.shape[1]
    keys, values = prefix_key_cache[0], prefix_value_cache[0]
    vmem = pl.BlockSpec(memory_space=pltpu.VMEM)
    hbm = pl.BlockSpec(memory_space=pl.ANY)
    f32, bf16 = jnp.float32, jnp.bfloat16
    links = 112
    dma = pltpu.SemaphoreType.DMA
    return pl.pallas_call(
        layer_kernel,
        out_shape=jax.ShapeDtypeStruct((2 * SUB, width), bf16),
        in_specs=[vmem] * 10 + [hbm] * 9,
        out_specs=vmem,
        scratch_shapes=[
            pltpu.VMEM(query_matrix.shape, bf16),
            pltpu.VMEM(key_matrix.shape, bf16),
            pltpu.VMEM(value_matrix.shape, bf16),
            pltpu.VMEM(keys.shape, bf16),
            pltpu.VMEM(values.shape, bf16),
            pltpu.VMEM((2, PEERS, CAP, cols), bf16),
            pltpu.VMEM((2, PEERS, CAP, cols), bf16),
            pltpu.VMEM((2, PEERS, CAP, cols), bf16),
            pltpu.VMEM((2, PEERS, CAP, cols), bf16),
            pltpu.VMEM((2, PEERS, 1, 128), f32),
            pltpu.VMEM((2, PEERS, 1, 128), f32),
            pltpu.VMEM(out_weight.shape, bf16),
            pltpu.VMEM((2, SPAN, width), f32),
            pltpu.VMEM((2, SPAN, width), bf16),
            pltpu.VMEM((2, 2, HALF, width), bf16),
            pltpu.VMEM((2, 2, HALF, width), bf16),
            pltpu.VMEM((2, 2, SUB, width), bf16),
            pltpu.VMEM((2, SUB, width), f32),
            pltpu.VMEM((RING, 2 * SPAN, width), bf16),
            pltpu.VMEM((4 * hidden, width), bf16),
            pltpu.VMEM((2 * hidden, width), bf16),
            pltpu.VMEM((RING, 2 * SPAN, width), bf16),
            pltpu.VMEM((2, 2, RING, HALF, width), bf16),
            pltpu.VMEM((2, 2, RING, HALF, width), bf16),
            pltpu.VMEM((2, 2, RING, SUB, width), bf16),
            pltpu.VMEM((2, 2, SUB, width), f32),
            pltpu.VMEM((2, RING, SUB, width), bf16),
            pltpu.VMEM((2, 2, HALF, width), bf16),
            pltpu.VMEM((2, 2, HALF, width), bf16),
            pltpu.VMEM((2, 2, SUB, width), bf16),
            dma((9,)),
            dma((2,)),
            dma((2, 2)),
            dma((2,)),
            dma((2, 2)),
            dma((2,)),
            dma((2, 2)),
            dma((3,)),
            dma((3,)),
            dma((links,)),
            dma((links,)),
        ],
        compiler_params=pltpu.CompilerParams(
            collective_id=0, has_side_effects=True, vmem_limit_bytes=60 << 20
        ),
        name="layer",
    )(
        states,
        attn_gain.reshape(-1, 128),
        query_gain[None],
        key_gain[None],
        segment[None],
        prefix_id[None],
        owner_map[None],
        post_gain.reshape(-1, 128),
        ffw_gain.reshape(-1, 128),
        post_ffw_gain.reshape(-1, 128),
        query_matrix,
        key_matrix,
        value_matrix,
        keys,
        values,
        out_weight,
        gate_weight.T,
        up_weight.T,
        down_weight,
    )


def solution(mesh):
    return jax.shard_map(
        body,
        mesh=mesh,
        in_specs=(
            P("req", None),
            P(),
            P(None, "mlp"),
            P(None, "mlp"),
            P(None, "mlp"),
            P(),
            P(),
            P("mlp", None),
            P(),
            P(),
            P(None, "req"),
            P(None, "req"),
            P("req", None),
            P(),
            P("req", None, "mlp"),
            P("req", None, "mlp"),
            P("req"),
            P("req"),
            P(),
        ),
        out_specs=P(("req", "mlp"), None),
        check_vma=False,
    )
```

```python
import jax
import jax.numpy as jnp
from jax import lax
from jax.experimental import pallas as pl
from jax.experimental.pallas import tpu as pltpu
from jax.sharding import PartitionSpec as P

EPS = 1e-06

MESH_ID = pl.DeviceIdType.MESH
RING = 4
SUB = 32
HALF = 16
CAP = 16
PEERS = 2 * RING * RING
PART = 16
SPAN = RING * SUB
ORDER = (2, 1, 3, 0)


def hops(offset):
    down, across = offset // (2 * RING), (offset // 2) % RING
    return min(down, RING - down) + min(across, RING - across)


FAR_FIRST = [
    sorted(range(max(start, 1), start + PART), key=lambda offset: -hops(offset))
    for start in range(0, PEERS, PART)
]


def normed(values_in, gain_vec):
    return (
        values_in
        * lax.rsqrt(jnp.mean(values_in * values_in, axis=-1, keepdims=True) + EPS)
        * gain_vec
    )


def layer_kernel(
    states_ref,
    attn_gain_ref,
    query_gain_ref,
    key_gain_ref,
    segment_ref,
    prefix_ref,
    owner_ref,
    post_gain_ref,
    ffw_gain_ref,
    last_gain_ref,
    query_w_ref,
    key_w_ref,
    value_w_ref,
    keys_ref,
    values_ref,
    out_w_ref,
    gate_ref,
    up_ref,
    down_ref,
    out_ref,
    query_w,
    key_w,
    value_w,
    stored_keys,
    stored_values,
    outgoing,
    incoming,
    results,
    back,
    log_out,
    log_back,
    out_w,
    projected,
    layer_out,
    layer_opposite,
    layer_merged,
    layer_side,
    residual,
    rows_buf,
    gate_up,
    down_w,
    partial,
    opposite_in,
    merged_out,
    side_in,
    row_sum,
    send2,
    opposite_in2,
    merged_out2,
    side_in2,
    local_sem,
    query_send_sem,
    query_recv_sem,
    back_send_sem,
    back_recv_sem,
    log_send_sem,
    log_recv_sem,
    weight_send,
    weight_recv,
    send_sem,
    recv_sem,
):
    me = lax.axis_index("req")
    layer = lax.axis_index("mlp")
    core = lax.rem(me, 2)
    chip = me // 2
    row, col = chip // RING, lax.rem(chip, RING)
    rows, width = states_ref.shape
    head = query_gain_ref.shape[1]
    heads = query_w.shape[1] // head
    cols = heads * head
    hidden = gate_ref.shape[0]
    quarter = 2 * SUB
    score_scale = head ** (-0.5)
    f32, bf16 = jnp.float32, jnp.bfloat16

    def shifted(offset, sign=1):
        down, across, flip = offset // (2 * RING), (offset // 2) % RING, offset % 2
        if sign < 0:
            down, across = (RING - down) % RING, (RING - across) % RING
        row_at = lax.rem(row + down, RING)
        col_at = lax.rem(col + across, RING)
        core_at = 1 - core if flip else core
        return ((row_at * RING + col_at) * 2 + core_at, layer)

    right, left, sibling = shifted(2), shifted(2, -1), shifted(1)
    upper, lower = shifted(2 * RING), shifted(2 * RING, -1)
    above = (me, lax.rem(layer + 1, RING))
    below = (me, lax.rem(layer + RING - 1, RING))

    barrier = pltpu.get_barrier_semaphore()
    for offset in range(1, PEERS):
        pl.semaphore_signal(barrier, inc=1, device_id=shifted(offset), device_id_type=MESH_ID)
    for peer in (above, below):
        pl.semaphore_signal(barrier, inc=1, device_id=peer, device_id_type=MESH_ID)

    sources = (gate_ref, up_ref, down_ref)
    targets = (
        gate_up.at[pl.ds(0, hidden)],
        gate_up.at[pl.ds(2 * hidden, hidden)],
        down_w.at[pl.ds(0, hidden)],
    )
    far_targets = (
        gate_up.at[pl.ds(hidden, hidden)],
        gate_up.at[pl.ds(3 * hidden, hidden)],
        down_w.at[pl.ds(hidden, hidden)],
    )
    local = []
    for index, (src, dst) in enumerate(
        (
            (query_w_ref, query_w),
            (key_w_ref, key_w),
            (value_w_ref, value_w),
            (keys_ref, stored_keys),
            (values_ref, stored_values),
            (out_w_ref, out_w),
        )
        + tuple(zip(sources, targets))
    ):
        copy = pltpu.make_async_copy(src, dst, local_sem.at[index])
        copy.start()
        local.append(copy)

    def line(ref):
        return jnp.concatenate([ref[i : i + 1] for i in range(ref.shape[0])], axis=1)

    normalized = normed(states_ref[...].astype(f32), line(attn_gain_ref)).astype(bf16)

    def column(values):
        return jnp.transpose(jnp.broadcast_to(values, (128, rows)))[:, :1]

    prefix_row = prefix_ref[...].astype(f32)
    prefix_col = column(prefix_row)
    row_at = lax.broadcasted_iota(jnp.int32, (rows, rows), 0)
    col_at = lax.broadcasted_iota(jnp.int32, (rows, rows), 1)
    same = jnp.where(
        (prefix_col == prefix_row) & (((row_at >> 3) & 1) == ((col_at >> 3) & 1)), 1.0, 0.0
    )
    rank_col = jnp.sum(jnp.where(col_at < row_at, same, 0.0), axis=1, keepdims=True)
    rank_row = jnp.sum(jnp.where(row_at < col_at, same, 0.0), axis=0, keepdims=True)
    groups = owner_ref.shape[1]
    onehot = prefix_col == lax.broadcasted_iota(jnp.int32, (rows, groups), 1).astype(f32)
    owner_col = jnp.sum(jnp.where(onehot, owner_ref[...].astype(f32), 0.0), axis=1, keepdims=True)
    owner_row = jnp.transpose(jnp.broadcast_to(owner_col, (rows, 128)))[:1]

    def place(owner, rank):
        owner = owner.astype(jnp.int32)
        down = ((owner >> 3) - row) & 3
        across = (((owner >> 1) & 3) - col) & 3
        flip = ((owner & 1) - core) & 1
        return (down * 8 + across * 2 + flip) * CAP + rank.astype(jnp.int32)

    place_col = place(owner_col, rank_col)
    place_row = place(owner_row, rank_row)
    set_row = (lax.broadcasted_iota(jnp.int32, (1, rows), 1) >> 3) & 1

    def of_set(values, group):
        count, lanes = values.shape
        return values.reshape(count // 16, 2, 8, lanes)[:, group].reshape(count // 2, lanes)

    local[0].wait()
    raw = jnp.dot(normalized, query_w[...], preferred_element_type=f32)
    queries = [
        normed(raw[:, g * head : (g + 1) * head], query_gain_ref[...]).astype(bf16)
        for g in range(heads)
    ]
    query_rows = jnp.concatenate(queries, axis=1)
    pl.semaphore_wait(barrier, PEERS + 1)
    slot_at = lax.broadcasted_iota(jnp.int32, (PART * CAP, rows), 0)
    def send_queries(group):
        goal = jnp.where(set_row == group, place_row, -1)
        for part in range(PEERS // PART):
            placing = jnp.where(slot_at + part * PART * CAP == goal, 1.0, 0.0).astype(bf16)
            packed = jnp.dot(placing, query_rows, preferred_element_type=f32).astype(bf16)
            packed = packed.reshape(PART, CAP, cols)
            if part == 0:
                incoming[group, 0] = packed[0]
            outgoing[group, pl.ds(part * PART, PART)] = packed
            for offset in FAR_FIRST[part]:
                pltpu.make_async_remote_copy(
                    src_ref=outgoing.at[group, offset],
                    dst_ref=incoming.at[group, offset],
                    send_sem=query_send_sem.at[group],
                    recv_sem=query_recv_sem.at[group, part],
                    device_id=shifted(offset),
                    device_id_type=MESH_ID,
                ).start()

    send_queries(0)
    weight_copies = []
    for index, (src, dst) in enumerate(zip(sources, far_targets)):
        copy = pltpu.make_async_remote_copy(
            src_ref=src,
            dst_ref=dst,
            send_sem=weight_send.at[index],
            recv_sem=weight_recv.at[index],
            device_id=sibling,
            device_id_type=MESH_ID,
        )
        copy.start()
        weight_copies.append(copy)

    local[1].wait()
    local[2].wait()
    raw = jnp.dot(normalized, key_w[...], preferred_element_type=f32)
    keys = normed(raw, key_gain_ref[...]).astype(bf16)
    values = jnp.dot(normalized, value_w[...], preferred_element_type=f32).astype(bf16)
    segment_row = segment_ref[...].astype(f32)
    allowed = (column(segment_row) == segment_row) & (row_at >= col_at)

    def attend(query, key, value, mask):
        scores = (
            lax.dot_general(query, key, (((1,), (1,)), ((), ())), preferred_element_type=f32)
            * score_scale
        )
        if mask is not None:
            scores = jnp.where(mask, scores, -jnp.inf)
        row_max = jnp.max(scores, axis=-1, keepdims=True)
        powers = jnp.exp(scores - row_max)
        total = jnp.sum(powers, axis=-1, keepdims=True)
        weights = (powers / total).astype(bf16)
        mixed = jnp.dot(weights, value, preferred_element_type=f32)
        return mixed, row_max + jnp.log(total)

    suffix = [attend(query, keys, values, allowed) for query in queries]
    send_queries(1)

    def remote_blocks(buf, group, part):
        start = max(part * PART, 1)
        return buf.at[group, pl.ds(start, (part + 1) * PART - start)]

    def await_blocks(buf, group, part, sem):
        blocks = remote_blocks(buf, group, part)
        pltpu.make_async_copy(blocks, blocks, sem).wait()

    local[3].wait()
    local[4].wait()
    lanes = lax.broadcasted_iota(jnp.int32, (PART * CAP, 128), 1)
    slot_of = lax.broadcasted_iota(jnp.int32, (PART * CAP, 128), 0) & (CAP - 1)
    def answer(group):
        for part in range(PEERS // PART):
            await_blocks(incoming, group, part, query_recv_sem.at[group, part])
            blocks = pl.ds(part * PART, PART)
            query = incoming[group, blocks].reshape(PART * CAP, cols)
            totals = jnp.zeros((PART * CAP, 128), f32)
            for g in range(heads):
                mixed, log_total = attend(
                    query[:, g * head : (g + 1) * head], stored_keys[...], stored_values[...], None
                )
                totals = jnp.where(lanes == CAP * g + slot_of, log_total, totals)
                results[group, blocks, :, pl.ds(g * head, head)] = mixed.astype(bf16).reshape(
                    PART, CAP, head
                )
            log_out[group, blocks] = jnp.sum(
                totals.reshape(PART, CAP, 128), axis=1, keepdims=True
            )

    def send_answers(group):
        for part in range(PEERS // PART):
            if part == 0:
                back[group, 0] = results[group, 0]
                log_back[group, 0] = log_out[group, 0]
            for offset in FAR_FIRST[part]:
                pltpu.make_async_remote_copy(
                    src_ref=results.at[group, offset],
                    dst_ref=back.at[group, offset],
                    send_sem=back_send_sem.at[group],
                    recv_sem=back_recv_sem.at[group, part],
                    device_id=shifted(offset, -1),
                    device_id_type=MESH_ID,
                ).start()
            for offset in FAR_FIRST[part]:
                pltpu.make_async_remote_copy(
                    src_ref=log_out.at[group, offset],
                    dst_ref=log_back.at[group, offset],
                    send_sem=log_send_sem.at[group],
                    recv_sem=log_recv_sem.at[group, part],
                    device_id=shifted(offset, -1),
                    device_id_type=MESH_ID,
                ).start()

    answer(0)
    send_answers(0)
    answer(1)
    blocks = results.at[0, pl.ds(1, PEERS - 1)]
    pltpu.make_async_copy(blocks, blocks, back_send_sem.at[0]).wait()
    send_answers(1)

    copies = []

    def send(src, dst, peer):
        index = len(copies)
        copy = pltpu.make_async_remote_copy(
            src_ref=src,
            dst_ref=dst,
            send_sem=send_sem.at[index],
            recv_sem=recv_sem.at[index],
            device_id=peer,
            device_id_type=MESH_ID,
        )
        copy.start()
        copies.append(copy)
        return copy

    def quarter_rows(ref, group, offset, start, size):
        at = lax.rem(layer + offset, RING) * SUB + start
        return ref.at[group, pl.ds(pl.multiple_of(at, HALF), size)]

    layer_opp, layer_plain, layer_far = {}, {}, {}

    def project(group):
        picked = jnp.zeros((rows // 2, cols), f32)
        places = of_set(place_col, group)
        for part in range(PEERS // PART):
            await_blocks(back, group, part, back_recv_sem.at[group, part])
            slots = lax.broadcasted_iota(jnp.int32, (rows // 2, PART * CAP), 1)
            choosing = jnp.where(slots + part * PART * CAP == places, 1.0, 0.0).astype(bf16)
            block = back[group, pl.ds(part * PART, PART)].reshape(PART * CAP, cols)
            picked = picked + jnp.dot(choosing, block, preferred_element_type=f32)
            await_blocks(log_back, group, part, log_recv_sem.at[group, part])
        peer_at = lax.broadcasted_iota(jnp.int32, (rows // 2, PEERS), 1)
        totals = jnp.dot(
            jnp.where(peer_at == places >> 4, 1.0, 0.0),
            log_back[group].reshape(PEERS, 128),
            precision=lax.Precision.HIGHEST,
            preferred_element_type=f32,
        )
        lane_at = lax.broadcasted_iota(jnp.int32, (rows // 2, 128), 1)
        attended = []
        for g in range(heads):
            mixed, log_total = suffix[g]
            prefix_lse = jnp.sum(
                jnp.where(lane_at == CAP * g + (places & (CAP - 1)), totals, 0.0),
                axis=1,
                keepdims=True,
            )
            blend = jax.nn.sigmoid(prefix_lse - of_set(log_total, group))
            attended.append(
                (
                    blend * picked[:, g * head : (g + 1) * head]
                    + (1.0 - blend) * of_set(mixed, group)
                ).astype(bf16)
            )
        out = jnp.dot(jnp.concatenate(attended, axis=1), out_w[...], preferred_element_type=f32)
        projected[group] = out
        layer_out[group] = out.astype(bf16)
        layer_opp[group] = (
            send(quarter_rows(layer_out, group, 2, 0, HALF), layer_opposite.at[0, group], above),
            send(quarter_rows(layer_out, group, 2, HALF, HALF), layer_opposite.at[1, group], below),
        )
        layer_plain[group] = (
            send(
                quarter_rows(layer_out, group, 1, HALF, HALF),
                layer_side.at[0, group, pl.ds(HALF, HALF)],
                above,
            ),
            send(
                quarter_rows(layer_out, group, 3, 0, HALF),
                layer_side.at[1, group, pl.ds(0, HALF)],
                below,
            ),
        )

    def merge_layers(group):
        layer_opp[group][0].wait_recv()
        layer_merged[0, group] = (
            quarter_rows(projected, group, 1, 0, HALF)[...] + layer_opposite[0, group].astype(f32)
        ).astype(bf16)
        a = send(layer_merged.at[0, group], layer_side.at[0, group, pl.ds(0, HALF)], above)
        layer_opp[group][1].wait_recv()
        layer_merged[1, group] = (
            quarter_rows(projected, group, 3, HALF, HALF)[...]
            + layer_opposite[1, group].astype(f32)
        ).astype(bf16)
        b = send(layer_merged.at[1, group], layer_side.at[1, group, pl.ds(HALF, HALF)], below)
        layer_far[group] = (a, b)

    first = ((right, left), (upper, lower))
    second = ((upper, lower), (right, left))
    step1, step2, across, relays = {}, {}, {}, {}

    def slot(group, chunk, sub, start=0, size=SUB):
        return rows_buf.at[chunk, pl.ds(group * SPAN + sub * SUB + start, size)]

    def send_across(group, sub):
        plus, minus = second[group]
        across[group, sub] = (
            send(slot(group, 0, sub), slot(group, 3, sub), plus),
            send(slot(group, 0, sub), slot(group, 1, sub), minus),
        )

    def relay_across(group, sub):
        plus, minus = second[group]
        across[group, sub][0].wait_recv()
        a = send(slot(group, 3, sub, 0, HALF), slot(group, 2, sub, 0, HALF), plus)
        across[group, sub][1].wait_recv()
        b = send(slot(group, 1, sub, HALF, HALF), slot(group, 2, sub, HALF, HALF), minus)
        relays[group, sub] = (a, b)

    def enter(group):
        for copy in layer_plain[group] + layer_far[group]:
            copy.wait_recv()
        total = (
            quarter_rows(projected, group, 0, 0, SUB)[...]
            + layer_side[0, group].astype(f32)
            + layer_side[1, group].astype(f32)
        )
        own = states_ref[pl.ds(pl.multiple_of(layer * quarter, quarter), quarter)].astype(f32)
        after = of_set(own, group) + normed(total, line(post_gain_ref))
        residual[group] = after
        rows_buf[0, pl.ds(group * SPAN, SUB)] = normed(after, line(ffw_gain_ref)).astype(bf16)
        plus, minus = first[group]
        step1[group] = (
            send(slot(group, 0, 0), slot(group, 0, 3), plus),
            send(slot(group, 0, 0), slot(group, 0, 1), minus),
        )
        send_across(group, 0)

    def spread(group):
        plus, minus = first[group]
        step1[group][0].wait_recv()
        a = send(slot(group, 0, 3, 0, HALF), slot(group, 0, 2, 0, HALF), plus)
        step1[group][1].wait_recv()
        b = send(slot(group, 0, 1, HALF, HALF), slot(group, 0, 2, HALF, HALF), minus)
        step2[group] = (a, b)
        send_across(group, 1)
        send_across(group, 3)

    def finish_spread(group):
        for copy in step2[group]:
            copy.wait_recv()
        send_across(group, 2)

    def compute(chunk, start, size):
        span = pl.ds(start, size)
        both = lax.dot_general(
            rows_buf[chunk, span],
            gate_up[...],
            (((1,), (1,)), ((), ())),
            preferred_element_type=f32,
        )
        gate = both[:, : 2 * hidden]
        act = (jax.nn.gelu(gate, approximate=True) * both[:, 2 * hidden :]).astype(bf16)
        partial[chunk, span] = jnp.dot(act, down_w[...], preferred_element_type=f32).astype(bf16)

    local[5].wait()
    project(0)
    merge_layers(0)
    enter(0)
    project(1)
    merge_layers(1)
    spread(0)
    relay_across(0, 0)
    enter(1)
    finish_spread(0)
    spread(1)
    relay_across(0, 1)
    relay_across(0, 3)
    relay_across(1, 0)
    finish_spread(1)
    for copy in local[6:]:
        copy.wait()
    for copy in weight_copies:
        copy.wait_recv()
    relay_across(0, 2)
    relay_across(1, 1)
    relay_across(1, 3)
    compute(0, 0, 2 * SPAN)
    relay_across(1, 2)
    compute(1, 0, 2 * SPAN)
    compute(3, 0, 2 * SPAN)

    opposite, plain, merged, last = {}, {}, {}, {}

    def piece(group, chunk, sub, start):
        return partial.at[chunk, pl.ds(group * SPAN + sub * SUB + start, HALF)]

    def side(group, which, sub, start):
        return side_in.at[which, group, sub, pl.ds(start, HALF)]

    def send_opposite(group):
        plus, minus = second[group]
        for sub in ORDER:
            opposite[group, sub] = (
                send(piece(group, 2, sub, 0), opposite_in.at[0, group, sub], plus),
                send(piece(group, 2, sub, HALF), opposite_in.at[1, group, sub], minus),
            )

    def send_plain(group):
        plus, minus = second[group]
        for sub in ORDER:
            plain[group, sub] = (
                send(piece(group, 1, sub, HALF), side(group, 0, sub, HALF), plus),
                send(piece(group, 3, sub, 0), side(group, 1, sub, 0), minus),
            )

    def merge(group, sub):
        plus, minus = second[group]
        opposite[group, sub][0].wait_recv()
        merged_out[0, group, sub] = (
            piece(group, 1, sub, 0)[...].astype(f32) + opposite_in[0, group, sub].astype(f32)
        ).astype(bf16)
        a = send(merged_out.at[0, group, sub], side(group, 0, sub, 0), plus)
        opposite[group, sub][1].wait_recv()
        merged_out[1, group, sub] = (
            piece(group, 3, sub, HALF)[...].astype(f32) + opposite_in[1, group, sub].astype(f32)
        ).astype(bf16)
        b = send(merged_out.at[1, group, sub], side(group, 1, sub, HALF), minus)
        merged[group, sub] = (a, b)

    def summed(group, sub):
        for copy in plain[group, sub] + merged[group, sub]:
            copy.wait_recv()
        return (
            partial[0, pl.ds(group * SPAN + sub * SUB, SUB)].astype(f32)
            + side_in[0, group, sub].astype(f32)
            + side_in[1, group, sub].astype(f32)
        )

    def turn_opposite(group):
        plus, minus = first[group]
        send2[group, 2] = summed(group, 2).astype(bf16)
        last[group, 0] = send(
            send2.at[group, 2, pl.ds(0, HALF)], opposite_in2.at[group, 0], plus
        )
        last[group, 1] = send(
            send2.at[group, 2, pl.ds(HALF, HALF)], opposite_in2.at[group, 1], minus
        )

    def turn_side(group, which):
        sub = (1, 3)[which]
        start = (HALF, 0)[which]
        row_sum[group, which] = summed(group, sub)
        send2[group, sub] = row_sum[group, which].astype(bf16)
        last[group, 2 + which] = send(
            send2.at[group, sub, pl.ds(start, HALF)],
            side_in2.at[group, which, pl.ds(start, HALF)],
            first[group][which],
        )

    def turn_merge(group, which):
        start = (0, HALF)[which]
        last[group, which].wait_recv()
        merged_out2[group, which] = (
            row_sum[group, which, pl.ds(start, HALF)] + opposite_in2[group, which].astype(f32)
        ).astype(bf16)
        last[group, 4 + which] = send(
            merged_out2.at[group, which],
            side_in2.at[group, which, pl.ds(start, HALF)],
            first[group][which],
        )

    def finish(group):
        own = summed(group, 0)
        for index in (2, 3, 4, 5):
            last[group, index].wait_recv()
        total = own + side_in2[group, 0].astype(f32) + side_in2[group, 1].astype(f32)
        return residual[group] + normed(total, line(last_gain_ref))

    for group in range(2):
        send_plain(group)
    for pair in relays.values():
        pair[0].wait_recv()
        pair[1].wait_recv()
    compute(2, 0, 2 * SPAN)
    for group in range(2):
        send_opposite(group)
    for sub in ORDER:
        merge(0, sub)
        merge(1, sub)
    for group in range(2):
        turn_opposite(group)
    for group in range(2):
        turn_side(group, 0)
        turn_side(group, 1)
    for group in range(2):
        turn_merge(group, 0)
        turn_merge(group, 1)
    ends = [finish(group).reshape(RING, 1, 8, width) for group in range(2)]
    out_ref[...] = jnp.concatenate(ends, axis=1).reshape(quarter, width).astype(out_ref.dtype)

    for group in range(2):
        for buf, sem in ((outgoing, query_send_sem), (log_out, log_send_sem)):
            blocks = buf.at[group, pl.ds(1, PEERS - 1)]
            pltpu.make_async_copy(blocks, blocks, sem.at[group]).wait()
    blocks = results.at[1, pl.ds(1, PEERS - 1)]
    pltpu.make_async_copy(blocks, blocks, back_send_sem.at[1]).wait()
    for copy in copies + weight_copies:
        copy.wait_send()


def body(
    states,
    attn_gain,
    query_matrix,
    key_matrix,
    value_matrix,
    query_gain,
    key_gain,
    out_weight,
    post_gain,
    ffw_gain,
    gate_weight,
    up_weight,
    down_weight,
    post_ffw_gain,
    prefix_key_cache,
    prefix_value_cache,
    segment,
    prefix_id,
    owner_map,
):
    rows, width = states.shape
    cols = query_matrix.shape[1]
    hidden = gate_weight.shape[1]
    keys, values = prefix_key_cache[0], prefix_value_cache[0]
    vmem = pl.BlockSpec(memory_space=pltpu.VMEM)
    hbm = pl.BlockSpec(memory_space=pl.ANY)
    f32, bf16 = jnp.float32, jnp.bfloat16
    links = 112
    dma = pltpu.SemaphoreType.DMA
    return pl.pallas_call(
        layer_kernel,
        out_shape=jax.ShapeDtypeStruct((2 * SUB, width), bf16),
        in_specs=[vmem] * 10 + [hbm] * 9,
        out_specs=vmem,
        scratch_shapes=[
            pltpu.VMEM(query_matrix.shape, bf16),
            pltpu.VMEM(key_matrix.shape, bf16),
            pltpu.VMEM(value_matrix.shape, bf16),
            pltpu.VMEM(keys.shape, bf16),
            pltpu.VMEM(values.shape, bf16),
            pltpu.VMEM((2, PEERS, CAP, cols), bf16),
            pltpu.VMEM((2, PEERS, CAP, cols), bf16),
            pltpu.VMEM((2, PEERS, CAP, cols), bf16),
            pltpu.VMEM((2, PEERS, CAP, cols), bf16),
            pltpu.VMEM((2, PEERS, 1, 128), f32),
            pltpu.VMEM((2, PEERS, 1, 128), f32),
            pltpu.VMEM(out_weight.shape, bf16),
            pltpu.VMEM((2, SPAN, width), f32),
            pltpu.VMEM((2, SPAN, width), bf16),
            pltpu.VMEM((2, 2, HALF, width), bf16),
            pltpu.VMEM((2, 2, HALF, width), bf16),
            pltpu.VMEM((2, 2, SUB, width), bf16),
            pltpu.VMEM((2, SUB, width), f32),
            pltpu.VMEM((RING, 2 * SPAN, width), bf16),
            pltpu.VMEM((4 * hidden, width), bf16),
            pltpu.VMEM((2 * hidden, width), bf16),
            pltpu.VMEM((RING, 2 * SPAN, width), bf16),
            pltpu.VMEM((2, 2, RING, HALF, width), bf16),
            pltpu.VMEM((2, 2, RING, HALF, width), bf16),
            pltpu.VMEM((2, 2, RING, SUB, width), bf16),
            pltpu.VMEM((2, 2, SUB, width), f32),
            pltpu.VMEM((2, RING, SUB, width), bf16),
            pltpu.VMEM((2, 2, HALF, width), bf16),
            pltpu.VMEM((2, 2, HALF, width), bf16),
            pltpu.VMEM((2, 2, SUB, width), bf16),
            dma((9,)),
            dma((2,)),
            dma((2, 2)),
            dma((2,)),
            dma((2, 2)),
            dma((2,)),
            dma((2, 2)),
            dma((3,)),
            dma((3,)),
            dma((links,)),
            dma((links,)),
        ],
        compiler_params=pltpu.CompilerParams(
            collective_id=0, has_side_effects=True, vmem_limit_bytes=60 << 20
        ),
        name="layer",
    )(
        states,
        attn_gain.reshape(-1, 128),
        query_gain[None],
        key_gain[None],
        segment[None],
        prefix_id[None],
        owner_map[None],
        post_gain.reshape(-1, 128),
        ffw_gain.reshape(-1, 128),
        post_ffw_gain.reshape(-1, 128),
        query_matrix,
        key_matrix,
        value_matrix,
        keys,
        values,
        out_weight,
        gate_weight.T,
        up_weight.T,
        down_weight,
    )


def solution(mesh):
    return jax.shard_map(
        body,
        mesh=mesh,
        in_specs=(
            P("req", None),
            P(),
            P(None, "mlp"),
            P(None, "mlp"),
            P(None, "mlp"),
            P(),
            P(),
            P("mlp", None),
            P(),
            P(),
            P(None, "req"),
            P(None, "req"),
            P("req", None),
            P(),
            P("req", None, "mlp"),
            P("req", None, "mlp"),
            P("req"),
            P("req"),
            P(),
        ),
        out_specs=P(("req", "mlp"), None),
        check_vma=False,
    )
```
